256 devices in a mesh: row: 16 (over x_lo, y, core), col: 16 (over x_hi, z).
Axes of the slice: x: 4 (x_hi: 2, x_lo: 2; x = x_hi * 2 + x_lo), y: 4, z: 8, core: 2. Of those that a mesh axis runs over, the one named last changes fastest.
Arguments:
- tokens: bfloat16 [512, 8192], P('col', 'row'), may hold values from -6 to 6
- cotangent: bfloat16 [512, 8192], P('col', 'row'), may hold values from -6 to 6
- gate_weight: bfloat16 [8192, 28672], P('row', 'col'), may hold values from -0.09375 to 0.09375
- up_weight: bfloat16 [8192, 28672], P('row', 'col'), may hold values from -0.09375 to 0.09375
- down_weight: bfloat16 [28672, 8192], P('col', 'row'), may hold values from -0.0625 to 0.0625
- gate_mask: int32 [64, 224], P('row', 'col'), may hold values 0 or 1
- up_mask: int32 [64, 224], P('row', 'col'), may hold values 0 or 1
- down_mask: int32 [224, 64], P('col', 'row'), may hold values 0 or 1
Outputs:
- output: bfloat16 [512, 8192], P('col', 'row')
- d_tokens: bfloat16 [512, 8192], P('col', 'row')
- grad_gate: bfloat16 [8192, 28672], P('row', 'col')
- grad_up: bfloat16 [8192, 28672], P('row', 'col')
- grad_down: bfloat16 [28672, 8192], P('col', 'row')
The draws below stay inside these ranges and needn't reach their ends.
Inputs may be any that keep to these rules, and one draw needn't show every extreme that they name: `gate_mask`: 1 keeps a block, 0 prunes it. `up_mask`: 1 keeps a block, 0 prunes it. `down_mask`: 1 keeps a block, 0 prunes it.
All inputs are finite; a program needn't handle non-finite values.
Results may differ from the reference program's by a relative error of at most 0.0049.
Values may be sent and summed in bfloat16 or wider, within the bound.
No kernel may reach another device: no remote copies, remote signals or barrier semaphores. Data moves between devices by JAX's collectives and lax.ppermute only.
A program may use at most 128 MiB of HBM per device.

```python
import jax
import jax.numpy as jnp

D = 8192
HID = 28672
BLK = 128
TOKENS = 512


def place_ends(drawn, own_key, least, high):
    index_at = [jax.random.randint(jax.random.fold_in(own_key, axis), (), 0, length) for axis, length in enumerate(drawn.shape)]
    widest = drawn.shape.index(max(drawn.shape))
    neighbour = index_at[:widest] + [(index_at[widest] + 1) % drawn.shape[widest]] + index_at[widest + 1:]
    return drawn.at[tuple(index_at)].set(least).at[tuple(neighbour)].set(high)


def shard_levels(stream_key, extent, pieces, least, largest):
    level = 1.0
    for position, shards_of in pieces:
        draws = jax.random.uniform(jax.random.fold_in(jax.random.fold_in(stream_key, 6), position), (shards_of,), jnp.float32, least / len(pieces), largest / len(pieces))
        level = level * jnp.repeat(jnp.exp(draws), extent[position] // shards_of).reshape((-1,) + (1,) * (len(extent) - 1 - position))
    return level


def bell_draw(stream_key, shape, spread, most, pieces=(), kind=jnp.bfloat16):
    result = jax.random.normal(stream_key, shape, jnp.float32) * spread
    if len(pieces) > 0:
        result = shard_levels(stream_key, shape, pieces, -0.22, 0.18) * result
    return jnp.clip(result, min=-most, max=most).astype(kind)


def setup_inputs(seed: int = 0) -> dict:
    streams_of = jax.random.split(jax.random.key(seed), 9)
    return {
        "tokens": bell_draw(streams_of[0], (TOKENS, D), 1.0, 6.0, ((0, 16), (1, 16))),
        "cotangent": bell_draw(streams_of[1], (TOKENS, D), 1.0, 6.0, ((0, 16), (1, 16))),
        "gate_weight": bell_draw(streams_of[2], (D, HID), (D // 2) ** -0.5, 0.09375, ((0, 16), (1, 16))),
        "up_weight": bell_draw(streams_of[3], (D, HID), (D // 2) ** -0.5, 0.09375, ((0, 16), (1, 16))),
        "down_weight": bell_draw(streams_of[4], (HID, D), (HID // 4) ** -0.5, 0.0625, ((0, 16), (1, 16))),
        "gate_mask": place_ends((jax.random.randint(streams_of[5], (D // BLK, HID // BLK), 0, 2) < 1).astype(jnp.int32), jax.random.fold_in(streams_of[5], 1), 0, 1),
        "up_mask": place_ends((jax.random.randint(streams_of[6], (D // BLK, HID // BLK), 0, 2) < 1).astype(jnp.int32), jax.random.fold_in(streams_of[6], 1), 0, 1),
        "down_mask": place_ends((jax.random.randint(streams_of[7], (HID // BLK, D // BLK), 0, 2) < 1).astype(jnp.int32), jax.random.fold_in(streams_of[7], 1), 0, 1),
    }


def masked(weight, block_mask):
    block_rows, block_cols = block_mask.shape
    total_rows, total_cols = weight.shape
    shaped = weight.reshape(block_rows, total_rows // block_rows, block_cols, total_cols // block_cols)
    return (shaped * block_mask.astype(weight.dtype)[:, None, :, None]).reshape(total_rows, total_cols)


def reference(tokens, cotangent, gate_weight, up_weight, down_weight, gate_mask, up_mask, down_mask):
    gate_eff = masked(gate_weight, gate_mask)
    up_eff = masked(up_weight, up_mask)
    down_eff = masked(down_weight, down_mask)
    gate = jnp.dot(tokens, gate_eff, preferred_element_type=jnp.float32)
    up = jnp.dot(tokens, up_eff, preferred_element_type=jnp.float32)
    sigmoid_gate = jax.nn.sigmoid(gate)
    activated = gate * sigmoid_gate
    hidden = (activated * up).astype(jnp.bfloat16)
    output = jnp.dot(hidden, down_eff, preferred_element_type=jnp.float32).astype(jnp.bfloat16)
    d_hidden = jnp.dot(cotangent, down_eff.T, preferred_element_type=jnp.float32)
    d_gate = (d_hidden * up * sigmoid_gate * (1.0 + gate * (1.0 - sigmoid_gate))).astype(jnp.bfloat16)
    d_up = (d_hidden * activated).astype(jnp.bfloat16)
    grad_down = masked(jnp.dot(hidden.T, cotangent, preferred_element_type=jnp.float32), down_mask).astype(jnp.bfloat16)
    grad_gate = masked(jnp.dot(tokens.T, d_gate, preferred_element_type=jnp.float32), gate_mask).astype(jnp.bfloat16)
    grad_up = masked(jnp.dot(tokens.T, d_up, preferred_element_type=jnp.float32), up_mask).astype(jnp.bfloat16)
    d_total = jnp.dot(d_gate, gate_eff.T, preferred_element_type=jnp.float32) + jnp.dot(d_up, up_eff.T, preferred_element_type=jnp.float32)
    d_tokens = d_total.astype(jnp.bfloat16)
    return (output, d_tokens, grad_gate, grad_up, grad_down)
```

```python
import jax
import jax.numpy as jnp
from jax import lax
from jax.sharding import Mesh
from jax.sharding import PartitionSpec as P

ROW = ("x_lo", "y", "core")
COL = ("x_hi", "z")
BF = jnp.bfloat16
F32 = jnp.float32


def masked(weight, block_mask):
    block_rows, block_cols = block_mask.shape
    total_rows, total_cols = weight.shape
    shaped = weight.reshape(
        block_rows, total_rows // block_rows, block_cols, total_cols // block_cols
    )
    return (shaped * block_mask.astype(weight.dtype)[:, None, :, None]).reshape(
        total_rows, total_cols
    )


def right_product(left, right):
    return lax.dot_general(left, right, (((1,), (1,)), ((), ())), preferred_element_type=F32)


def left_product(left, right):
    return lax.dot_general(left, right, (((0,), (0,)), ((), ())), preferred_element_type=F32)


def swap(array, axis):
    return lax.ppermute(array, axis, [(0, 1), (1, 0)])


def per_device(
    tokens, cotangent, gate_weight, up_weight, down_weight, gate_mask, up_mask, down_mask
):
    width = tokens.shape[1]
    hid = gate_weight.shape[1]
    share = tokens.shape[0]
    col_n = lax.axis_size(COL)
    pair_n = lax.axis_size(("x_lo", "y"))
    core = lax.axis_index("core")
    gate_eff = masked(gate_weight, gate_mask)
    up_eff = masked(up_weight, up_mask)
    down_eff = masked(down_weight, down_mask)

    both = jnp.concatenate([tokens, cotangent], axis=1)
    both_all = lax.all_to_all(
        jnp.broadcast_to(both, (col_n,) + both.shape), COL, 0, 0, tiled=True
    ).reshape(col_n * share, 2 * width)
    rows_all = both_all[:, :width]
    cot_all = both_all[:, width:]

    parts = jnp.concatenate(
        [
            jnp.dot(rows_all, gate_eff, preferred_element_type=F32),
            jnp.dot(rows_all, up_eff, preferred_element_type=F32),
            right_product(cot_all, down_eff),
        ],
        axis=1,
    ).reshape(pair_n, 2, share, 3 * hid)
    kept = lax.dynamic_index_in_dim(parts, core, 1, keepdims=False)
    given = lax.dynamic_index_in_dim(parts, 1 - core, 1, keepdims=False).astype(BF)
    pair_sum = (kept + swap(given, "core").astype(F32)).astype(BF)
    sums = jnp.sum(
        lax.all_to_all(pair_sum, ("x_lo", "y"), 0, 0, tiled=True).astype(F32), axis=0
    )
    gate, up, hidden_grad = sums[:, :hid], sums[:, hid : 2 * hid], sums[:, 2 * hid :]

    sigmoid_gate = jax.nn.sigmoid(gate)
    activated = gate * sigmoid_gate
    hidden = (activated * up).astype(BF)
    gate_grad = (
        hidden_grad * up * sigmoid_gate * (1.0 + gate * (1.0 - sigmoid_gate))
    ).astype(BF)
    up_grad = (hidden_grad * activated).astype(BF)

    mine = jnp.concatenate([hidden, gate_grad, up_grad], axis=1)
    own_half = lax.all_to_all(
        jnp.broadcast_to(mine, (pair_n,) + mine.shape), ("x_lo", "y"), 0, 0, tiled=True
    )
    other_half = swap(own_half, "core")
    first = jnp.where(core == 0, own_half, other_half)
    second = jnp.where(core == 0, other_half, own_half)
    acts = jnp.stack([first, second], axis=1).reshape(col_n * share, 3 * hid)
    hidden_all, gate_grad_all, up_grad_all = (
        acts[:, :hid],
        acts[:, hid : 2 * hid],
        acts[:, 2 * hid :],
    )

    output_part = jnp.dot(hidden_all, down_eff, preferred_element_type=F32)
    tokens_part = right_product(gate_grad_all, gate_eff) + right_product(up_grad_all, up_eff)
    out_parts = jnp.concatenate([output_part, tokens_part], axis=1).astype(BF)
    out_sums = jnp.sum(
        lax.all_to_all(
            out_parts.reshape(col_n, share, 2 * width), COL, 0, 0, tiled=True
        ).astype(F32),
        axis=0,
    ).astype(BF)
    output, d_tokens = out_sums[:, :width], out_sums[:, width:]

    grad_down = masked(left_product(hidden_all, cot_all), down_mask).astype(BF)
    grad_gate = masked(left_product(rows_all, gate_grad_all), gate_mask).astype(BF)
    grad_up = masked(left_product(rows_all, up_grad_all), up_mask).astype(BF)
    return (output, d_tokens, grad_gate, grad_up, grad_down)


def solution(mesh):
    fine = Mesh(mesh.devices.reshape(2, 4, 2, 2, 8), ROW + COL)
    in_specs = (
        P(COL, ROW),
        P(COL, ROW),
        P(ROW, COL),
        P(ROW, COL),
        P(COL, ROW),
        P(ROW, COL),
        P(ROW, COL),
        P(COL, ROW),
    )
    out_specs = (P(COL, ROW), P(COL, ROW), P(ROW, COL), P(ROW, COL), P(COL, ROW))
    return jax.shard_map(
        per_device, mesh=fine, in_specs=in_specs, out_specs=out_specs, check_vma=False
    )
```

```python
import jax
import jax.numpy as jnp
from jax import lax
from jax.experimental import pallas as pl
from jax.experimental.pallas import tpu as pltpu
from jax.sharding import Mesh
from jax.sharding import PartitionSpec as P


ROW = ("x_lo", "y", "core")
COL = ("x_hi", "z")
PAIR = ("x_lo", "y")
BF = jnp.bfloat16
F32 = jnp.float32
BLK = 128


def prepare_kernel(*refs):
    for weight, mask, eff, full in zip(refs[0:3], refs[3:6], refs[6:9], refs[9:12]):
        for i in range(mask.shape[0]):
            rows = pl.ds(i * BLK, BLK)
            keep = jnp.broadcast_to(mask[pl.ds(i, 1), :], (BLK, mask.shape[1])).astype(BF)
            full[rows, :] = keep
            eff[rows, :] = weight[rows, :] * keep


def prepare(weights, masks):
    wide = [jnp.repeat(mask.astype(F32), BLK, axis=1) for mask in masks]
    shapes = [jax.ShapeDtypeStruct(weight.shape, BF) for weight in weights]
    outs = pl.pallas_call(
        prepare_kernel,
        out_shape=shapes + shapes,
        in_specs=[pl.BlockSpec(memory_space=pltpu.VMEM)] * 6,
        out_specs=[pl.BlockSpec(memory_space=pltpu.VMEM)] * 6,
        name="prepare",
    )(*weights, *wide)
    return outs[:3], outs[3:]


def dot(left, right):
    return jnp.dot(left, right, preferred_element_type=F32)


def right_product(left, right):
    return lax.dot_general(left, right, (((1,), (1,)), ((), ())), preferred_element_type=F32)


def left_product(left, right):
    return lax.dot_general(left, right, (((0,), (0,)), ((), ())), preferred_element_type=F32)


def swap(array):
    return lax.ppermute(array, "core", [(0, 1), (1, 0)])


def gather(array, axes):
    copies = jnp.broadcast_to(array, (lax.axis_size(axes),) + array.shape)
    return lax.all_to_all(copies, axes, 0, 0, tiled=True)


def exchange(array, axes):
    parts = lax.axis_size(axes)
    split = array.reshape((parts, array.shape[0] // parts) + array.shape[1:])
    return lax.all_to_all(split, axes, 0, 0, tiled=True)


def send_down(array, axis, hops):
    size = lax.axis_size(axis)
    return lax.ppermute(array, axis, [(i, (i - hops) % size) for i in range(size)])


def arrange_kernel(place, *refs):
    parts, out = refs[:-1], refs[-1]
    size = len(parts)
    rows = parts[0].shape[1]
    for k, part in enumerate(parts):
        start = pl.multiple_of(lax.rem(place[0] + k, size) * rows, rows)
        out[:, pl.ds(start, rows), :] = part[...]


def arrange(place, parts):
    halves, rows, width = parts[0].shape
    return pl.pallas_call(
        arrange_kernel,
        out_shape=jax.ShapeDtypeStruct((halves, len(parts) * rows, width), BF),
        in_specs=[pl.BlockSpec(memory_space=pltpu.SMEM)]
        + [pl.BlockSpec(memory_space=pltpu.VMEM)] * len(parts),
        out_specs=pl.BlockSpec(memory_space=pltpu.VMEM),
        name="arrange",
    )(place, *parts)


def gather_by_permutes(array):
    high, z = lax.axis_index("x_hi"), lax.axis_index("z")
    size = lax.axis_size("z")
    facing = send_down(array, "x_hi", 1)
    pair = jnp.stack([jnp.where(high == 0, array, facing), jnp.where(high == 0, facing, array)])
    got = [pair] + [send_down(pair, "z", k) for k in range(1, size)]
    return arrange(z.reshape(1).astype(jnp.int32), got)


def exchange_by_permutes(kept, given, share):
    z = lax.axis_index("z")
    size = lax.axis_size("z")
    arrived = send_down(given, "x_hi", 1)
    parts = (kept + arrived.astype(F32)).reshape(size, share, -1)
    result = lax.dynamic_index_in_dim(parts, z, 0, keepdims=False)
    parts = parts.astype(BF)
    away = [
        lax.dynamic_index_in_dim(parts, (z + size - k) % size, 0, keepdims=False)
        for k in range(1, size)
    ]
    for k in range(1, size):
        result = result + send_down(away[k - 1], "z", k).astype(F32)
    return result


def layer(
    tokens, cotangent, gate_weight, up_weight, down_weight, gate_mask, up_mask, down_mask
):
    share, width = tokens.shape
    hid = gate_weight.shape[1]
    core = lax.axis_index("core")
    high = lax.axis_index("x_hi")

    def halves(gathered):
        split = gathered.reshape(2, -1, width)
        own = lax.dynamic_index_in_dim(split, core, 0, keepdims=False)
        other = lax.dynamic_index_in_dim(split, 1 - core, 0, keepdims=False)
        return own, other

    rows_all = gather(tokens, COL)
    (gate_eff, up_eff, down_eff), (gate_full, up_full, down_full) = prepare(
        (gate_weight, up_weight, down_weight), (gate_mask, up_mask, down_mask)
    )

    rows_own, rows_other = halves(rows_all)
    gate_recv = swap(dot(rows_other, gate_eff))
    up_recv = swap(dot(rows_other, up_eff))
    gate_pair = (dot(rows_own, gate_eff) + gate_recv).astype(BF)
    up_pair = (dot(rows_own, up_eff) + up_recv).astype(BF)
    gate_up = jnp.concatenate([gate_pair, up_pair], axis=1)
    gate_up, cot_in = lax.optimization_barrier((gate_up, cotangent))
    sums = jnp.sum(exchange(gate_up, PAIR).astype(F32), axis=0)
    gate, up = sums[:, :hid], sums[:, hid:]

    cot_own, cot_other = halves(gather_by_permutes(cot_in))
    back_recv = swap(right_product(cot_other, down_eff))
    back_pair = (right_product(cot_own, down_eff) + back_recv).astype(BF)

    sigmoid_gate = jax.nn.sigmoid(gate)
    activated = gate * sigmoid_gate
    hidden = (activated * up).astype(BF)
    hidden_own = gather(hidden, PAIR).reshape(-1, hid)
    hidden_own, back_pair = lax.optimization_barrier((hidden_own, back_pair))
    hidden_other = swap(hidden_own)

    back_got = exchange(back_pair, PAIR)
    hidden_grad = jnp.sum(back_got.astype(F32), axis=0)
    gate_grad = (
        hidden_grad * up * sigmoid_gate * (1.0 + gate * (1.0 - sigmoid_gate))
    ).astype(BF)
    up_grad = (hidden_grad * activated).astype(BF)
    both_grads = jnp.concatenate([gate_grad, up_grad], axis=1)
    grads_own = gather(both_grads, PAIR).reshape(-1, 2 * hid)
    grads_other = swap(grads_own)

    output_own, output_other = dot(hidden_own, down_eff), dot(hidden_other, down_eff)
    output_kept = jnp.where(core == high, output_own, output_other)
    output_given = jnp.where(core == high, output_other, output_own).astype(BF)
    output = exchange_by_permutes(output_kept, output_given, share).astype(BF)

    def back(grads):
        return right_product(grads[:, :hid], gate_eff) + right_product(grads[:, hid:], up_eff)

    back_own, back_other = back(grads_own), back(grads_other)
    tokens_part = jnp.concatenate(
        [jnp.where(core == 0, back_own, back_other), jnp.where(core == 0, back_other, back_own)],
        axis=0,
    ).astype(BF)
    tokens_got = exchange(tokens_part, COL)
    d_tokens = jnp.sum(tokens_got.astype(F32), axis=0).astype(BF)

    rows_local = jnp.concatenate([rows_own, rows_other], axis=0)
    cot_local = jnp.concatenate([cot_own, cot_other], axis=0)
    hidden_local = jnp.concatenate([hidden_own, hidden_other], axis=0)
    grads_local = jnp.concatenate([grads_own, grads_other], axis=0)
    grad_down = (left_product(hidden_local, cot_local) * down_full.astype(F32)).astype(BF)
    grad_gate = (left_product(rows_local, grads_local[:, :hid]) * gate_full.astype(F32)).astype(BF)
    grad_up = (
        left_product(rows_local, grads_local[:, hid:]) * up_full.astype(F32)
    ).astype(BF)
    return (output, d_tokens, grad_gate, grad_up, grad_down)


def solution(mesh):
    fine = Mesh(mesh.devices.reshape(2, 4, 2, 2, 8), ROW + COL)
    in_specs = (
        P(COL, ROW),
        P(COL, ROW),
        P(ROW, COL),
        P(ROW, COL),
        P(COL, ROW),
        P(ROW, COL),
        P(ROW, COL),
        P(COL, ROW),
    )
    out_specs = (P(COL, ROW), P(COL, ROW), P(ROW, COL), P(ROW, COL), P(COL, ROW))
    return jax.shard_map(layer, mesh=fine, in_specs=in_specs, out_specs=out_specs, check_vma=False)
```

```python
import jax
import jax.numpy as jnp
from jax import lax
from jax.experimental import pallas as pl
from jax.experimental.pallas import tpu as pltpu
from jax.sharding import Mesh
from jax.sharding import PartitionSpec as P


ROW = ("x_lo", "y", "core")
COL = ("x_hi", "z")
PAIR = ("x_lo", "y")
BF = jnp.bfloat16
F32 = jnp.float32
BLK = 128
STEP = 256


def local_call(kernel, outs, *args):
    whole = pl.BlockSpec(memory_space=pltpu.VMEM)
    single = not isinstance(outs, list)
    return pl.pallas_call(
        kernel,
        out_shape=outs,
        in_specs=[whole] * len(args),
        out_specs=whole if single else [whole] * len(outs),
    )(*args)


def nn(left, right):
    return jnp.dot(left, right, preferred_element_type=F32)


def nt(left, right):
    return lax.dot_general(left, right, (((1,), (1,)), ((), ())), preferred_element_type=F32)


def prepare_kernel(*refs):
    for weight, mask, eff in zip(refs[0:3], refs[3:6], refs[6:9]):
        for i in range(mask.shape[0]):
            rows = pl.ds(i * BLK, BLK)
            keep = jnp.broadcast_to(mask[pl.ds(i, 1), :], (BLK, mask.shape[1])).astype(BF)
            eff[rows, :] = weight[rows, :] * keep


def partial_kernel(own, cross, gate, up, down, gate_x, up_x, down_x, out):
    width = gate.shape[0]
    hid = gate.shape[1]
    rows, rows_x = own[:, :width], cross[:, :width]
    cot, cot_x = own[:, width:], cross[:, width:]
    for j in range(hid // STEP):
        cols = pl.ds(j * STEP, STEP)
        out[:, cols] = (nn(rows, gate[:, cols]) + nn(rows_x, gate_x[:, cols])).astype(BF)
        out[:, pl.ds(hid + j * STEP, STEP)] = (
            nn(rows, up[:, cols]) + nn(rows_x, up_x[:, cols])
        ).astype(BF)
        out[:, pl.ds(2 * hid + j * STEP, STEP)] = (
            nt(cot, down[cols, :]) + nt(cot_x, down_x[cols, :])
        ).astype(BF)


def activation_kernel(got, out):
    copies = got.shape[0]
    hid = got.shape[2] // 3

    def total(start):
        cols = pl.ds(start, STEP)
        acc = got[0, :, cols].astype(F32)
        for i in range(1, copies):
            acc = acc + got[i, :, cols].astype(F32)
        return acc

    for j in range(hid // STEP):
        starts = [part * hid + j * STEP for part in range(3)]
        gate, up, d_hidden = [total(start) for start in starts]
        sigmoid = jax.nn.sigmoid(gate)
        activated = gate * sigmoid
        values = (
            activated * up,
            d_hidden * up * sigmoid * (1.0 + gate * (1.0 - sigmoid)),
            d_hidden * activated,
        )
        for start, value in zip(starts, values):
            rounded = value.astype(BF)
            for i in range(copies):
                out[i, :, pl.ds(start, STEP)] = rounded


def result_kernel(acts, gate, up, down, out):
    hid = gate.shape[1]
    width = gate.shape[0]
    out[:, :width] = nn(acts[:, :hid], down[...]).astype(BF)
    out[:, width:] = (
        nt(acts[:, hid : 2 * hid], gate[...]) + nt(acts[:, 2 * hid :], up[...])
    ).astype(BF)


def gradient_kernel(acts, acts_x, own, other, *refs):
    masks, (grad_gate, grad_up, grad_down) = refs[:3], refs[3:]
    width, hid = grad_gate.shape
    rows, rows_x = own[:, :width].T, other[:, :width].T
    cot, cot_x = own[:, width:], other[:, width:]
    for j in range(hid // STEP):
        for part, mask, grad in ((1, masks[0], grad_gate), (2, masks[1], grad_up)):
            cols = pl.ds(part * hid + j * STEP, STEP)
            here = pl.ds(j * STEP, STEP)
            value = nn(rows, acts[:, cols]) + nn(rows_x, acts_x[:, cols])
            for i in range(width // BLK):
                keep = mask[pl.ds(i, 1), here]
                grad[pl.ds(i * BLK, BLK), here] = (value[i * BLK : (i + 1) * BLK] * keep).astype(BF)
        cols = pl.ds(j * STEP, STEP)
        value = nn(acts[:, cols].T, cot) + nn(acts_x[:, cols].T, cot_x)
        for i in range(STEP // BLK):
            keep = masks[2][pl.ds(j * (STEP // BLK) + i, 1), :]
            grad_down[pl.ds(j * STEP + i * BLK, BLK), :] = (
                value[i * BLK : (i + 1) * BLK] * keep
            ).astype(BF)


def swap(array):
    return lax.ppermute(array, "core", [(0, 1), (1, 0)])


def layer(
    tokens, cotangent, gate_weight, up_weight, down_weight, gate_mask, up_mask, down_mask
):
    share, width = tokens.shape
    hid = gate_weight.shape[1]
    core = lax.axis_index("core")
    pairs = lax.axis_size(PAIR)
    cols = lax.axis_size(COL)
    half = share // 2

    both = jnp.concatenate([tokens, cotangent], axis=1)
    gathered = lax.all_to_all(
        jnp.broadcast_to(both, (cols,) + both.shape), COL, 0, 0, tiled=True
    )
    weights = (gate_weight, up_weight, down_weight)
    shapes = [jax.ShapeDtypeStruct(weight.shape, BF) for weight in weights]
    wide = [
        jnp.repeat(mask.astype(F32), BLK, axis=1) for mask in (gate_mask, up_mask, down_mask)
    ]
    effs = local_call(prepare_kernel, shapes, *weights, *wide)
    effs_x = [swap(eff) for eff in effs]

    own = lax.dynamic_slice_in_dim(gathered, core * half, half, 1).reshape(-1, 2 * width)
    other = lax.dynamic_slice_in_dim(gathered, (1 - core) * half, half, 1).reshape(-1, 2 * width)
    cross = swap(other)
    parts = local_call(
        partial_kernel,
        jax.ShapeDtypeStruct((own.shape[0], 3 * hid), BF),
        own,
        cross,
        *effs,
        *effs_x,
    ).reshape(pairs, -1, 3 * hid)
    got = lax.all_to_all(parts, PAIR, 0, 0, tiled=True)
    copies = local_call(activation_kernel, jax.ShapeDtypeStruct(got.shape, BF), got)
    acts = lax.all_to_all(copies, PAIR, 0, 0, tiled=True).reshape(-1, 3 * hid)

    result_shape = jax.ShapeDtypeStruct((acts.shape[0], 2 * width), BF)
    away = swap(local_call(result_kernel, result_shape, acts, *effs_x))
    here = local_call(result_kernel, result_shape, acts, *effs)
    send = jnp.concatenate(
        [here.reshape(cols, half, 2 * width), away.reshape(cols, half, 2 * width)], axis=1
    )
    arrived = lax.all_to_all(send, COL, 0, 0, tiled=True)
    sums = jnp.sum(arrived.astype(F32), axis=0)
    first, second = sums[:half], sums[half:]
    sums = jnp.concatenate(
        [jnp.where(core == 0, first, second), jnp.where(core == 0, second, first)], axis=0
    ).astype(BF)
    output, d_tokens = sums[:, :width], sums[:, width:]

    send, acts_late = lax.optimization_barrier((send, acts))
    acts_x = swap(acts_late)
    grad_gate, grad_up, grad_down = local_call(
        gradient_kernel, shapes, acts_late, acts_x, own, other, *wide
    )
    return (output, d_tokens, grad_gate, grad_up, grad_down)


def solution(mesh):
    fine = Mesh(mesh.devices.reshape(2, 4, 2, 2, 8), ROW + COL)
    in_specs = (
        P(COL, ROW),
        P(COL, ROW),
        P(ROW, COL),
        P(ROW, COL),
        P(COL, ROW),
        P(ROW, COL),
        P(ROW, COL),
        P(COL, ROW),
    )
    out_specs = (P(COL, ROW), P(COL, ROW), P(ROW, COL), P(ROW, COL), P(COL, ROW))
    return jax.shard_map(layer, mesh=fine, in_specs=in_specs, out_specs=out_specs, check_vma=False)
```

```python
import jax
import jax.numpy as jnp
from jax import lax
from jax.experimental import pallas as pl
from jax.experimental.pallas import tpu as pltpu
from jax.sharding import Mesh
from jax.sharding import PartitionSpec as P


ROW = ("x_lo", "y", "core")
COL = ("x_hi", "z")
PAIR = ("x_lo", "y")
BF = jnp.bfloat16
F32 = jnp.float32
BLK = 128
STEP = 256


def local_call(kernel, outs, *args):
    whole = pl.BlockSpec(memory_space=pltpu.VMEM)
    single = not isinstance(outs, list)
    return pl.pallas_call(
        kernel,
        out_shape=outs,
        in_specs=[whole] * len(args),
        out_specs=whole if single else [whole] * len(outs),
    )(*args)


def nn(left, right):
    return jnp.dot(left, right, preferred_element_type=F32)


def nt(left, right):
    return lax.dot_general(left, right, (((1,), (1,)), ((), ())), preferred_element_type=F32)


def prepare_kernel(*refs):
    for weight, mask, eff in zip(refs[0:3], refs[3:6], refs[6:9]):
        for i in range(mask.shape[0]):
            rows = pl.ds(i * BLK, BLK)
            keep = jnp.broadcast_to(mask[pl.ds(i, 1), :], (BLK, mask.shape[1])).astype(BF)
            eff[rows, :] = weight[rows, :] * keep


def partial_sums(place, own, cross, effs, effs_x):
    gate = effs[0]
    tokens, both = own.shape
    width, hid = gate.shape
    share = tokens // place.shape[0]

    def kernel(place, own, cross, gate, up, down, gate_x, up_x, down_x, *refs):
        outs, (left, left_x) = refs[:-2], refs[-2:]

        @pl.when(pl.program_id(0) == 0)
        def _():
            for r in range(len(outs)):
                source = pl.ds(pl.multiple_of(place[r] * share, share), share)
                left[pl.ds(r * share, share), :] = own[source, :]
                left_x[pl.ds(r * share, share), :] = cross[source, :]

        values = (
            nn(left[:, :width], gate[...]) + nn(left_x[:, :width], gate_x[...]),
            nn(left[:, :width], up[...]) + nn(left_x[:, :width], up_x[...]),
            nt(left[:, width:], down[...]) + nt(left_x[:, width:], down_x[...]),
        )
        for part, value in enumerate(values):
            for r, out in enumerate(outs):
                out[part] = value[r * share : (r + 1) * share].astype(out.dtype)

    wide = pl.BlockSpec((width, STEP), lambda j: (0, j))
    tall = pl.BlockSpec((STEP, width), lambda j: (j, 0))
    fixed = pl.BlockSpec((tokens, both), lambda j: (0, 0))
    shape = (3, share, hid)
    return pl.pallas_call(
        kernel,
        out_shape=[
            jax.ShapeDtypeStruct(shape, F32 if r == 0 else BF) for r in range(place.shape[0])
        ],
        grid=(hid // STEP,),
        in_specs=[pl.BlockSpec(memory_space=pltpu.SMEM), fixed, fixed]
        + [wide, wide, tall, wide, wide, tall],
        out_specs=[pl.BlockSpec((3, share, STEP), lambda j: (0, 0, j))] * place.shape[0],
        scratch_shapes=[pltpu.VMEM((tokens, both), BF)] * 2,
        name="partial_sums",
    )(place, own, cross, *effs, *effs_x)


def activation_kernel(*refs):
    got, out = refs[:-1], refs[-1]
    hid = out.shape[2]
    for j in range(hid // STEP):
        cols = pl.ds(j * STEP, STEP)
        sums = []
        for part in range(3):
            acc = got[0][part, :, cols]
            for ref in got[1:]:
                acc = acc + ref[part, :, cols].astype(F32)
            sums.append(acc)
        gate, up, d_hidden = sums
        sigmoid = jax.nn.sigmoid(gate)
        activated = gate * sigmoid
        out[0, :, cols] = (activated * up).astype(BF)
        out[1, :, cols] = (
            d_hidden * up * sigmoid * (1.0 + gate * (1.0 - sigmoid))
        ).astype(BF)
        out[2, :, cols] = (d_hidden * activated).astype(BF)


def results(acts, gate, up, down, out):
    width = gate.shape[0]
    out[:, :width] = nn(acts[0], down[...]).astype(BF)
    out[:, width:] = (nt(acts[1], gate[...]) + nt(acts[2], up[...])).astype(BF)


def result_kernel(acts, gate, up, down, out):
    results(acts, gate, up, down, out)


def arrange_kernel(place, *refs):
    shares, (gate, up, down), (acts, out) = refs[:10], refs[10:13], refs[13:]
    share = shares[0].shape[1]
    hid = acts.shape[2]
    full = (0, 1, 3, 4, 5, 7)
    for r, ref in zip(full, shares[:6]):
        rows = pl.ds(pl.multiple_of(place[r] * share, share), share)
        acts[:, rows, :] = ref[...]
    for r, first, second in ((2, shares[6], shares[7]), (6, shares[8], shares[9])):
        rows = pl.ds(pl.multiple_of(place[r] * share, share), share)
        acts[:, rows, : hid // 2] = first[...]
        acts[:, rows, hid // 2 :] = second[...]
    results(acts, gate, up, down, out)


def gradient_kernel(acts, acts_x, own, other, *refs):
    masks, (grad_gate, grad_up, grad_down) = refs[:3], refs[3:]
    width, hid = grad_gate.shape
    rows, rows_x = own[:, :width].T, other[:, :width].T
    cot, cot_x = own[:, width:], other[:, width:]
    for j in range(hid // STEP):
        here = pl.ds(j * STEP, STEP)
        for part, mask, grad in ((1, masks[0], grad_gate), (2, masks[1], grad_up)):
            value = nn(rows, acts[part, :, here]) + nn(rows_x, acts_x[part, :, here])
            for i in range(width // BLK):
                keep = mask[pl.ds(i, 1), here]
                grad[pl.ds(i * BLK, BLK), here] = (value[i * BLK : (i + 1) * BLK] * keep).astype(BF)
        value = nn(acts[0, :, here].T, cot) + nn(acts_x[0, :, here].T, cot_x)
        for i in range(STEP // BLK):
            keep = masks[2][pl.ds(j * (STEP // BLK) + i, 1), :]
            grad_down[pl.ds(j * STEP + i * BLK, BLK), :] = (
                value[i * BLK : (i + 1) * BLK] * keep
            ).astype(BF)


def swap(array):
    return lax.ppermute(array, "core", [(0, 1), (1, 0)])


def layer(
    tokens, cotangent, gate_weight, up_weight, down_weight, gate_mask, up_mask, down_mask
):
    share, width = tokens.shape
    hid = gate_weight.shape[1]
    core = lax.axis_index("core")
    pairs = lax.axis_size(PAIR)
    cols = lax.axis_size(COL)
    half = share // 2

    both = jnp.concatenate([tokens, cotangent], axis=1)
    gathered = lax.all_to_all(
        jnp.broadcast_to(both, (cols,) + both.shape), COL, 0, 0, tiled=True
    )
    weights = (gate_weight, up_weight, down_weight)
    shapes = [jax.ShapeDtypeStruct(weight.shape, BF) for weight in weights]
    wide = [
        jnp.repeat(mask.astype(F32), BLK, axis=1) for mask in (gate_mask, up_mask, down_mask)
    ]
    effs = local_call(prepare_kernel, shapes, *weights, *wide)
    effs_x = [swap(eff) for eff in effs]

    own = lax.dynamic_slice_in_dim(gathered, core * half, half, 1).reshape(-1, 2 * width)
    other = lax.dynamic_slice_in_dim(gathered, (1 - core) * half, half, 1).reshape(-1, 2 * width)
    cross = swap(other)
    x_lo, y = lax.axis_index("x_lo"), lax.axis_index("y")
    y_n = lax.axis_size("y")
    place = jnp.stack(
        [(x_lo ^ (r // y_n)) * y_n + (y + r % y_n) % y_n for r in range(pairs)]
    ).astype(jnp.int32)
    parts = partial_sums(place, own, cross, effs, effs_x)

    got = {0: parts[0]}
    for r in (6, 5, 7, 2, 4, 1, 3):
        moves = [
            (i, ((i // y_n) ^ (r // y_n)) * y_n + (i % y_n + r % y_n) % y_n)
            for i in range(pairs)
        ]
        got[r] = lax.ppermute(parts[r], PAIR, moves)
    mine = local_call(
        activation_kernel,
        jax.ShapeDtypeStruct((3, parts[0].shape[1], hid), BF),
        *[got[r] for r in range(pairs)],
    )

    def from_up(array):
        return lax.ppermute(array, "y", [(i, (i - 1) % y_n) for i in range(y_n)])

    def from_down(array):
        return lax.ppermute(array, "y", [(i, (i + 1) % y_n) for i in range(y_n)])

    mid = hid // 2
    up_one, down_one = from_up(mine), from_down(mine)
    facing = lax.ppermute(mine, "x_lo", [(0, 1), (1, 0)])
    far = [from_up(up_one[:, :, :mid]), from_down(down_one[:, :, mid:])]
    facing_up, facing_down = from_up(facing), from_down(facing)
    far = far + [from_up(facing_up[:, :, :mid]), from_down(facing_down[:, :, mid:])]

    tokens_n = own.shape[0]
    result_shape = jax.ShapeDtypeStruct((tokens_n, 2 * width), BF)
    acts, away = pl.pallas_call(
        arrange_kernel,
        out_shape=[jax.ShapeDtypeStruct((3, tokens_n, hid), BF), result_shape],
        in_specs=[pl.BlockSpec(memory_space=pltpu.SMEM)]
        + [pl.BlockSpec(memory_space=pltpu.VMEM)] * 13,
        out_specs=[pl.BlockSpec(memory_space=pltpu.VMEM)] * 2,
        name="arrange",
    )(place, mine, up_one, down_one, facing, facing_up, facing_down, *far, *effs_x)
    away = swap(away)
    here = local_call(result_kernel, result_shape, acts, *effs)
    send = jnp.concatenate(
        [here.reshape(cols, half, 2 * width), away.reshape(cols, half, 2 * width)], axis=1
    )
    arrived = lax.all_to_all(send, COL, 0, 0, tiled=True)
    sums = jnp.sum(arrived.astype(F32), axis=0)
    first, second = sums[:half], sums[half:]
    sums = jnp.concatenate(
        [jnp.where(core == 0, first, second), jnp.where(core == 0, second, first)], axis=0
    ).astype(BF)
    output, d_tokens = sums[:, :width], sums[:, width:]

    send, acts_late = lax.optimization_barrier((send, acts))
    acts_x = swap(acts_late)
    grad_gate, grad_up, grad_down = local_call(
        gradient_kernel, shapes, acts_late, acts_x, own, other, *wide
    )
    return (output, d_tokens, grad_gate, grad_up, grad_down)


def solution(mesh):
    fine = Mesh(mesh.devices.reshape(2, 4, 2, 2, 8), ROW + COL)
    in_specs = (
        P(COL, ROW),
        P(COL, ROW),
        P(ROW, COL),
        P(ROW, COL),
        P(COL, ROW),
        P(ROW, COL),
        P(ROW, COL),
        P(COL, ROW),
    )
    out_specs = (P(COL, ROW), P(COL, ROW), P(ROW, COL), P(ROW, COL), P(COL, ROW))
    return jax.shard_map(layer, mesh=fine, in_specs=in_specs, out_specs=out_specs, check_vma=False)
```

```python
import jax
import jax.numpy as jnp
from jax import lax
from jax.experimental import pallas as pl
from jax.experimental.pallas import tpu as pltpu
from jax.sharding import Mesh
from jax.sharding import PartitionSpec as P


ROW = ("x_lo", "y", "core")
COL = ("x_hi", "z")
PAIR = ("x_lo", "y")
BF = jnp.bfloat16
F32 = jnp.float32
BLK = 128
STEP = 256


def local_call(kernel, outs, *args):
    whole = pl.BlockSpec(memory_space=pltpu.VMEM)
    single = not isinstance(outs, list)
    return pl.pallas_call(
        kernel,
        out_shape=outs,
        in_specs=[whole] * len(args),
        out_specs=whole if single else [whole] * len(outs),
    )(*args)


def nn(left, right):
    return jnp.dot(left, right, preferred_element_type=F32)


def nt(left, right):
    return lax.dot_general(left, right, (((1,), (1,)), ((), ())), preferred_element_type=F32)


def prepare_kernel(weight, mask, eff):
    for i in range(mask.shape[0]):
        rows = pl.ds(i * BLK, BLK)
        keep = jnp.broadcast_to(mask[pl.ds(i, 1), :], (BLK, mask.shape[1])).astype(BF)
        eff[rows, :] = weight[rows, :] * keep


def split_kernel(place, *refs):
    chunks, (own, other) = refs[:-2], refs[-2:]
    half = chunks[0].shape[0] // 2
    core = place[len(chunks)]
    for i, chunk in enumerate(chunks):
        rows = pl.ds(pl.multiple_of(place[i] * half, half), half)
        own[rows, :] = chunk[pl.ds(pl.multiple_of(core * half, half), half), :]
        other[rows, :] = chunk[pl.ds(pl.multiple_of((1 - core) * half, half), half), :]


def partial_sums(place, own, cross, effs, effs_x):
    gate = effs[0]
    tokens, both = own.shape
    width, hid = gate.shape
    chips = place.shape[0]
    y_n = chips // 2
    share = tokens // chips
    half = share // 2
    order = [(r, 0) for r in range(chips)]
    order += [(x * y_n + y, 1) for y in range(y_n) for x in range(2)]
    groups = [y_n * half, y_n * half] + [2 * half] * y_n
    dtypes = [F32, BF, F32] + [BF] * (y_n - 1)

    def kernel(place, own, cross, gate, up, down, gate_x, up_x, down_x, *refs):
        outs, (left, left_x) = refs[:-2], refs[-2:]

        @pl.when(pl.program_id(0) == 0)
        def _():
            for i, (r, part) in enumerate(order):
                source = pl.ds(pl.multiple_of(place[r] * share + part * half, half), half)
                left[pl.ds(i * half, half), :] = own[source, :]
                left_x[pl.ds(i * half, half), :] = cross[source, :]

        values = (
            nn(left[:, :width], gate[...]) + nn(left_x[:, :width], gate_x[...]),
            nn(left[:, :width], up[...]) + nn(left_x[:, :width], up_x[...]),
            nt(left[:, width:], down[...]) + nt(left_x[:, width:], down_x[...]),
        )
        for part, value in enumerate(values):
            start = 0
            for rows, out in zip(groups, outs):
                out[part] = value[start : start + rows].astype(out.dtype)
                start += rows

    wide = pl.BlockSpec((width, STEP), lambda j: (0, j))
    tall = pl.BlockSpec((STEP, width), lambda j: (j, 0))
    fixed = pl.BlockSpec((tokens, both), lambda j: (0, 0))
    return pl.pallas_call(
        kernel,
        out_shape=[jax.ShapeDtypeStruct((3, n, hid), t) for n, t in zip(groups, dtypes)],
        grid=(hid // STEP,),
        in_specs=[pl.BlockSpec(memory_space=pltpu.SMEM), fixed, fixed]
        + [wide, wide, tall, wide, wide, tall],
        out_specs=[pl.BlockSpec((3, n, STEP), lambda j: (0, 0, j)) for n in groups],
        scratch_shapes=[pltpu.VMEM((tokens, both), BF)] * 2,
        name="partial_sums",
    )(place, own, cross, *effs, *effs_x)


def middle_kernel(x_kept, x_got, y_kept, *refs):
    y_got, outs = refs[:3], refs[3:]
    half = outs[0].shape[1]
    for i, out in enumerate(outs[:4]):
        rows = pl.ds(i * half, half)
        out[...] = (x_kept[:, rows, :] + x_got[:, rows, :].astype(F32)).astype(out.dtype)
    for i, out in enumerate(outs[4:]):
        rows = pl.ds(i * half, half)
        total = y_kept[:, rows, :]
        for ref in y_got:
            total = total + ref[:, rows, :].astype(F32)
        out[...] = total.astype(out.dtype)


def activation_kernel(x_kept, x_one, x_two, x_three, y_kept, y_one, out):
    hid = out.shape[2]
    half = x_kept.shape[1]
    for row, kept, got in ((0, x_kept, (x_one, x_two, x_three)), (half, y_kept, (y_one,))):
        rows = pl.ds(row, half)
        for j in range(hid // STEP):
            cols = pl.ds(j * STEP, STEP)
            sums = []
            for part in range(3):
                acc = kept[part, :, cols]
                for ref in got:
                    acc = acc + ref[part, :, cols].astype(F32)
                sums.append(acc)
            gate, up, d_hidden = sums
            sigmoid = jax.nn.sigmoid(gate)
            activated = gate * sigmoid
            out[0, rows, cols] = (activated * up).astype(BF)
            out[1, rows, cols] = (
                d_hidden * up * sigmoid * (1.0 + gate * (1.0 - sigmoid))
            ).astype(BF)
            out[2, rows, cols] = (d_hidden * activated).astype(BF)


def results(acts, gate, up, down, out):
    width = gate.shape[0]
    out[:, :width] = nn(acts[0], down[...]).astype(BF)
    out[:, width:] = (nt(acts[1], gate[...]) + nt(acts[2], up[...])).astype(BF)


def result_kernel(acts, gate, up, down, out):
    results(acts, gate, up, down, out)


def arrange_kernel(place, *refs):
    shares, (gate, up, down), (acts, out) = refs[:10], refs[10:13], refs[13:]
    share = shares[0].shape[1]
    hid = acts.shape[2]
    full = (0, 1, 3, 4, 5, 7)
    for r, ref in zip(full, shares[:6]):
        rows = pl.ds(pl.multiple_of(place[r] * share, share), share)
        acts[:, rows, :] = ref[...]
    for r, first, second in ((2, shares[6], shares[7]), (6, shares[8], shares[9])):
        rows = pl.ds(pl.multiple_of(place[r] * share, share), share)
        acts[:, rows, : hid // 2] = first[...]
        acts[:, rows, hid // 2 :] = second[...]
    results(acts, gate, up, down, out)


def gradient_kernel(acts, acts_x, own, other, *refs):
    masks, (grad_gate, grad_up, grad_down) = refs[:3], refs[3:]
    width, hid = grad_gate.shape
    rows, rows_x = own[:, :width].T, other[:, :width].T
    cot, cot_x = own[:, width:], other[:, width:]
    for j in range(hid // STEP):
        here = pl.ds(j * STEP, STEP)
        for part, mask, grad in ((1, masks[0], grad_gate), (2, masks[1], grad_up)):
            value = nn(rows, acts[part, :, here]) + nn(rows_x, acts_x[part, :, here])
            for i in range(width // BLK):
                keep = mask[pl.ds(i, 1), here]
                grad[pl.ds(i * BLK, BLK), here] = (value[i * BLK : (i + 1) * BLK] * keep).astype(BF)
        value = nn(acts[0, :, here].T, cot) + nn(acts_x[0, :, here].T, cot_x)
        for i in range(STEP // BLK):
            keep = masks[2][pl.ds(j * (STEP // BLK) + i, 1), :]
            grad_down[pl.ds(j * STEP + i * BLK, BLK), :] = (
                value[i * BLK : (i + 1) * BLK] * keep
            ).astype(BF)


def swap(array):
    return lax.ppermute(array, "core", [(0, 1), (1, 0)])


def layer(
    tokens, cotangent, gate_weight, up_weight, down_weight, gate_mask, up_mask, down_mask
):
    share, width = tokens.shape
    hid = gate_weight.shape[1]
    core = lax.axis_index("core")
    pairs = lax.axis_size(PAIR)
    cols = lax.axis_size(COL)
    half = share // 2

    high, z = lax.axis_index("x_hi"), lax.axis_index("z")
    z_n = lax.axis_size("z")

    def along(axis, array, hops):
        n = lax.axis_size(axis)
        return lax.ppermute(array, axis, [(i, (i - hops) % n) for i in range(n)])

    both = jnp.concatenate([tokens, cotangent], axis=1)
    pair = jnp.stack([both, along("x_hi", both, 1)])
    ups, downs = [pair], [pair]
    for _ in range(1, z_n // 2):
        ups.append(along("z", ups[-1], 1))
        downs.append(along("z", downs[-1], -1))
    chunks = [(0, 0, both), (1, 0, pair[1])]
    for k in range(1, z_n // 2):
        for rel in range(2):
            chunks += [(rel, k, ups[k][rel]), (rel, z_n - k, downs[k][rel])]
    chunks += [(0, z_n // 2, along("z", ups[-1][0], 1)), (1, z_n // 2, along("z", downs[-1][1], -1))]
    order = jnp.stack(
        [(high ^ rel) * z_n + (z + k) % z_n for rel, k, _ in chunks] + [core]
    ).astype(jnp.int32)

    weights = (gate_weight, up_weight, down_weight)
    shapes = [jax.ShapeDtypeStruct(weight.shape, BF) for weight in weights]
    wide = [
        jnp.repeat(mask.astype(F32), BLK, axis=1) for mask in (gate_mask, up_mask, down_mask)
    ]
    effs = [local_call(prepare_kernel, *args) for args in zip(shapes, weights, wide)]
    effs_x = [swap(eff) for eff in effs]

    own_shape = jax.ShapeDtypeStruct((cols * half, 2 * width), BF)
    own, other = pl.pallas_call(
        split_kernel,
        out_shape=[own_shape, own_shape],
        in_specs=[pl.BlockSpec(memory_space=pltpu.SMEM)]
        + [pl.BlockSpec(memory_space=pltpu.VMEM)] * len(chunks),
        out_specs=[pl.BlockSpec(memory_space=pltpu.VMEM)] * 2,
        name="split",
    )(order, *[chunk for _, _, chunk in chunks])
    cross = swap(other)
    x_lo, y = lax.axis_index("x_lo"), lax.axis_index("y")
    y_n = lax.axis_size("y")
    place = jnp.stack(
        [(x_lo ^ (r // y_n)) * y_n + (y + r % y_n) % y_n for r in range(pairs)]
    ).astype(jnp.int32)
    parts = partial_sums(place, own, cross, effs, effs_x)

    x_kept, x_given, y_kept = parts[:3]
    quarter = [
        jax.ShapeDtypeStruct((3, x_kept.shape[1] // y_n, hid), t) for t in (F32, BF, BF, BF, F32, BF)
    ]
    mids = local_call(
        middle_kernel,
        quarter,
        x_kept,
        along("x_lo", x_given, 1),
        y_kept,
        *[along("y", parts[2 + k], -k) for k in (1, 2, 3)],
    )
    mine = local_call(
        activation_kernel,
        jax.ShapeDtypeStruct((3, 2 * quarter[0].shape[1], hid), BF),
        mids[0],
        *[along("y", mids[k], -k) for k in (1, 2, 3)],
        mids[4],
        along("x_lo", mids[5], 1),
    )

    def from_up(array):
        return lax.ppermute(array, "y", [(i, (i - 1) % y_n) for i in range(y_n)])

    def from_down(array):
        return lax.ppermute(array, "y", [(i, (i + 1) % y_n) for i in range(y_n)])

    mid = hid // 2
    up_one, down_one = from_up(mine), from_down(mine)
    facing = lax.ppermute(mine, "x_lo", [(0, 1), (1, 0)])
    far = [from_up(up_one[:, :, :mid]), from_down(down_one[:, :, mid:])]
    facing_up, facing_down = from_up(facing), from_down(facing)
    far = far + [from_up(facing_up[:, :, :mid]), from_down(facing_down[:, :, mid:])]

    tokens_n = own.shape[0]
    result_shape = jax.ShapeDtypeStruct((tokens_n, 2 * width), BF)
    acts, away = pl.pallas_call(
        arrange_kernel,
        out_shape=[jax.ShapeDtypeStruct((3, tokens_n, hid), BF), result_shape],
        in_specs=[pl.BlockSpec(memory_space=pltpu.SMEM)]
        + [pl.BlockSpec(memory_space=pltpu.VMEM)] * 13,
        out_specs=[pl.BlockSpec(memory_space=pltpu.VMEM)] * 2,
        name="arrange",
    )(place, mine, up_one, down_one, facing, facing_up, facing_down, *far, *effs_x)
    away = swap(away)
    here = local_call(result_kernel, result_shape, acts, *effs)
    send = jnp.concatenate(
        [here.reshape(cols, half, 2 * width), away.reshape(cols, half, 2 * width)], axis=1
    )
    arrived = lax.all_to_all(send, COL, 0, 0, tiled=True)
    sums = jnp.sum(arrived.astype(F32), axis=0)
    first, second = sums[:half], sums[half:]
    sums = jnp.concatenate(
        [jnp.where(core == 0, first, second), jnp.where(core == 0, second, first)], axis=0
    ).astype(BF)
    output, d_tokens = sums[:, :width], sums[:, width:]

    send, acts_late = lax.optimization_barrier((send, acts))
    acts_x = swap(acts_late)
    grad_gate, grad_up, grad_down = local_call(
        gradient_kernel, shapes, acts_late, acts_x, own, other, *wide
    )
    return (output, d_tokens, grad_gate, grad_up, grad_down)


def solution(mesh):
    fine = Mesh(mesh.devices.reshape(2, 4, 2, 2, 8), ROW + COL)
    in_specs = (
        P(COL, ROW),
        P(COL, ROW),
        P(ROW, COL),
        P(ROW, COL),
        P(COL, ROW),
        P(ROW, COL),
        P(ROW, COL),
        P(COL, ROW),
    )
    out_specs = (P(COL, ROW), P(COL, ROW), P(ROW, COL), P(ROW, COL), P(COL, ROW))
    return jax.shard_map(layer, mesh=fine, in_specs=in_specs, out_specs=out_specs, check_vma=False)
```

```python
import jax
import jax.numpy as jnp
from jax import lax
from jax.experimental import pallas as pl
from jax.experimental.pallas import tpu as pltpu
from jax.sharding import Mesh
from jax.sharding import PartitionSpec as P


ROW = ("x_lo", "y", "core")
COL = ("x_hi", "z")
PAIR = ("x_lo", "y")
BF = jnp.bfloat16
F32 = jnp.float32
BLK = 128
STEP = 256


def local_call(kernel, mib, outs, *args, place=None, scratch=(), far=0):
    whole = pl.BlockSpec(memory_space=pltpu.VMEM)
    single = not isinstance(outs, list)
    first = [] if place is None else [place]
    specs = [whole] * (len(args) - far) + [pl.BlockSpec(memory_space=pl.ANY)] * far
    return pl.pallas_call(
        kernel,
        out_shape=outs,
        in_specs=[pl.BlockSpec(memory_space=pltpu.SMEM)] * len(first) + specs,
        out_specs=whole if single else [whole] * len(outs),
        scratch_shapes=scratch,
        compiler_params=pltpu.CompilerParams(vmem_limit_bytes=mib << 20),
    )(*first, *args)


def nn(left, right):
    return jnp.dot(left, right, preferred_element_type=F32)


def nt(left, right):
    return lax.dot_general(left, right, (((1,), (1,)), ((), ())), preferred_element_type=F32)


def prepare_kernel(*refs):
    for weight, mask, eff in zip(refs[0:3], refs[3:6], refs[6:9]):
        for i in range(mask.shape[0]):
            rows = pl.ds(i * BLK, BLK)
            keep = jnp.broadcast_to(mask[pl.ds(i, 1), :], (BLK, mask.shape[1])).astype(BF)
            eff[rows, :] = weight[rows, :] * keep


def partial_sums(place, own, cross, effs, effs_x):
    gate = effs[0]
    tokens, both = own.shape
    width, hid = gate.shape
    chips = place.shape[0]
    share = tokens // chips

    def kernel(place, own, cross, *refs):
        sources, outs, (left, left_x), held, sems = (
            refs[:6],
            refs[6 : 6 + chips],
            refs[6 + chips : 8 + chips],
            refs[8 + chips : 14 + chips],
            refs[14 + chips],
        )
        copies = [
            pltpu.make_async_copy(source, hold, sems.at[i])
            for i, (source, hold) in enumerate(zip(sources, held))
        ]
        for copy in copies:
            copy.start()
        for r in range(chips):
            source = pl.ds(pl.multiple_of(place[r] * share, share), share)
            left[pl.ds(r * share, share), :] = own[source, :]
            left_x[pl.ds(r * share, share), :] = cross[source, :]
        for part in range(3):
            copies[2 * part].wait()
            copies[2 * part + 1].wait()
            weight, weight_x = held[2 * part], held[2 * part + 1]
            for j in range(hid // STEP):
                here = pl.ds(j * STEP, STEP)
                if part < 2:
                    value = nn(left[:, :width], weight[:, here])
                    value += nn(left_x[:, :width], weight_x[:, here])
                else:
                    value = nt(left[:, width:], weight[here, :])
                    value += nt(left_x[:, width:], weight_x[here, :])
                for r, out in enumerate(outs):
                    out[part, :, here] = value[r * share : (r + 1) * share].astype(out.dtype)

    outs = [jax.ShapeDtypeStruct((3, share, hid), F32 if r == 0 else BF) for r in range(chips)]
    weights = [weight for two in zip(effs, effs_x) for weight in two]
    scratch = [pltpu.VMEM((tokens, both), BF)] * 2
    scratch += [pltpu.VMEM(weight.shape, BF) for weight in weights]
    scratch += [pltpu.SemaphoreType.DMA((6,))]
    return local_call(kernel, 24, outs, own, cross, *weights, place=place, scratch=scratch, far=6)


def activation_kernel(*refs):
    got, out = refs[:-1], refs[-1]
    hid = out.shape[2]
    for j in range(hid // STEP):
        cols = pl.ds(j * STEP, STEP)
        sums = []
        for part in range(3):
            acc = got[0][part, :, cols]
            for ref in got[1:]:
                acc = acc + ref[part, :, cols].astype(F32)
            sums.append(acc)
        gate, up, d_hidden = sums
        sigmoid = jax.nn.sigmoid(gate)
        activated = gate * sigmoid
        out[0, :, cols] = (activated * up).astype(BF)
        out[1, :, cols] = (
            d_hidden * up * sigmoid * (1.0 + gate * (1.0 - sigmoid))
        ).astype(BF)
        out[2, :, cols] = (d_hidden * activated).astype(BF)


def results(acts, weights, out, held, sems, ahead=lambda: None):
    copies = [
        pltpu.make_async_copy(weight, hold, sems.at[i])
        for i, (weight, hold) in enumerate(zip(weights, held))
    ]
    for copy in copies:
        copy.start()
    ahead()
    down, gate, up = held
    width = gate.shape[0]
    copies[0].wait()
    out[:, :width] = nn(acts[0], down[...]).astype(BF)
    copies[1].wait()
    value = nt(acts[1], gate[...])
    copies[2].wait()
    out[:, width:] = (value + nt(acts[2], up[...])).astype(BF)


def result_kernel(acts, down, gate, up, out, *refs):
    results(acts, (down, gate, up), out, refs[:3], refs[3])


def arrange_kernel(place, *refs):
    shares, weights, (acts, out), held, sems = (
        refs[:10],
        refs[10:13],
        refs[13:15],
        refs[15:18],
        refs[18],
    )
    share = shares[0].shape[1]
    hid = acts.shape[2]
    full = (0, 1, 3, 4, 5, 7)

    def ahead():
        for r, ref in zip(full, shares[:6]):
            rows = pl.ds(pl.multiple_of(place[r] * share, share), share)
            acts[:, rows, :] = ref[...]
        for r, first, second in ((2, shares[6], shares[7]), (6, shares[8], shares[9])):
            rows = pl.ds(pl.multiple_of(place[r] * share, share), share)
            acts[:, rows, : hid // 2] = first[...]
            acts[:, rows, hid // 2 :] = second[...]

    results(acts, weights, out, held, sems, ahead)


def gradient_kernel(acts, acts_x, own, other, *refs):
    masks, (grad_gate, grad_up, grad_down) = refs[:3], refs[3:]
    width, hid = grad_gate.shape
    rows, rows_x = own[:, :width].T, other[:, :width].T
    cot, cot_x = own[:, width:], other[:, width:]
    for j in range(hid // STEP):
        here = pl.ds(j * STEP, STEP)
        for part, mask, grad in ((1, masks[0], grad_gate), (2, masks[1], grad_up)):
            value = nn(rows, acts[part, :, here]) + nn(rows_x, acts_x[part, :, here])
            for i in range(width // BLK):
                keep = mask[pl.ds(i, 1), here]
                grad[pl.ds(i * BLK, BLK), here] = (value[i * BLK : (i + 1) * BLK] * keep).astype(BF)
        value = nn(acts[0, :, here].T, cot) + nn(acts_x[0, :, here].T, cot_x)
        for i in range(STEP // BLK):
            keep = masks[2][pl.ds(j * (STEP // BLK) + i, 1), :]
            grad_down[pl.ds(j * STEP + i * BLK, BLK), :] = (
                value[i * BLK : (i + 1) * BLK] * keep
            ).astype(BF)


def swap(array):
    return lax.ppermute(array, "core", [(0, 1), (1, 0)])


def layer(
    tokens, cotangent, gate_weight, up_weight, down_weight, gate_mask, up_mask, down_mask
):
    share, width = tokens.shape
    hid = gate_weight.shape[1]
    core = lax.axis_index("core")
    pairs = lax.axis_size(PAIR)
    cols = lax.axis_size(COL)
    half = share // 2

    both = jnp.concatenate([tokens, cotangent], axis=1)
    gathered = lax.all_to_all(
        jnp.broadcast_to(both, (cols,) + both.shape), COL, 0, 0, tiled=True
    )
    weights = (gate_weight, up_weight, down_weight)
    shapes = [jax.ShapeDtypeStruct(weight.shape, BF) for weight in weights]
    wide = [
        jnp.repeat(mask.astype(F32), BLK, axis=1) for mask in (gate_mask, up_mask, down_mask)
    ]
    effs = local_call(prepare_kernel, 20, shapes, *weights, *wide)
    effs_x = [swap(eff) for eff in effs]

    own = lax.dynamic_slice_in_dim(gathered, core * half, half, 1).reshape(-1, 2 * width)
    other = lax.dynamic_slice_in_dim(gathered, (1 - core) * half, half, 1).reshape(-1, 2 * width)
    cross = swap(other)
    x_lo, y = lax.axis_index("x_lo"), lax.axis_index("y")
    y_n = lax.axis_size("y")
    place = jnp.stack(
        [(x_lo ^ (r // y_n)) * y_n + (y + r % y_n) % y_n for r in range(pairs)]
    ).astype(jnp.int32)
    parts = partial_sums(place, own, cross, effs, effs_x)

    got = {0: parts[0]}
    for r in (6, 5, 7, 2, 4, 1, 3):
        moves = [
            (i, ((i // y_n) ^ (r // y_n)) * y_n + (i % y_n + r % y_n) % y_n)
            for i in range(pairs)
        ]
        got[r] = lax.ppermute(parts[r], PAIR, moves)
    mine = local_call(
        activation_kernel,
        12,
        jax.ShapeDtypeStruct((3, parts[0].shape[1], hid), BF),
        *[got[r] for r in range(pairs)],
    )

    def from_up(array):
        return lax.ppermute(array, "y", [(i, (i - 1) % y_n) for i in range(y_n)])

    def from_down(array):
        return lax.ppermute(array, "y", [(i, (i + 1) % y_n) for i in range(y_n)])

    mid = hid // 2
    up_one, down_one = from_up(mine), from_down(mine)
    facing = lax.ppermute(mine, "x_lo", [(0, 1), (1, 0)])
    far = [from_up(up_one[:, :, :mid]), from_down(down_one[:, :, mid:])]
    facing_up, facing_down = from_up(facing), from_down(facing)
    far = far + [from_up(facing_up[:, :, :mid]), from_down(facing_down[:, :, mid:])]

    tokens_n = own.shape[0]
    result_shape = jax.ShapeDtypeStruct((tokens_n, 2 * width), BF)
    fetch = [pltpu.VMEM(shapes[i].shape, BF) for i in (2, 0, 1)] + [pltpu.SemaphoreType.DMA((3,))]
    acts, away = local_call(
        arrange_kernel,
        16,
        [jax.ShapeDtypeStruct((3, tokens_n, hid), BF), result_shape],
        mine,
        up_one,
        down_one,
        facing,
        facing_up,
        facing_down,
        *far,
        effs_x[2],
        *effs_x[:2],
        place=place,
        scratch=fetch,
        far=3,
    )
    away = swap(away)
    here = local_call(
        result_kernel, 12, result_shape, acts, effs[2], *effs[:2], scratch=fetch, far=3
    )
    send = jnp.concatenate(
        [here.reshape(cols, half, 2 * width), away.reshape(cols, half, 2 * width)], axis=1
    )
    arrived = lax.all_to_all(send, COL, 0, 0, tiled=True)
    sums = jnp.sum(arrived.astype(F32), axis=0)
    first, second = sums[:half], sums[half:]
    sums = jnp.concatenate(
        [jnp.where(core == 0, first, second), jnp.where(core == 0, second, first)], axis=0
    ).astype(BF)
    output, d_tokens = sums[:, :width], sums[:, width:]

    send, acts_late = lax.optimization_barrier((send, acts))
    acts_x = swap(acts_late)
    grad_gate, grad_up, grad_down = local_call(
        gradient_kernel, 20, shapes, acts_late, acts_x, own, other, *wide
    )
    return (output, d_tokens, grad_gate, grad_up, grad_down)


def solution(mesh):
    fine = Mesh(mesh.devices.reshape(2, 4, 2, 2, 8), ROW + COL)
    in_specs = (
        P(COL, ROW),
        P(COL, ROW),
        P(ROW, COL),
        P(ROW, COL),
        P(COL, ROW),
        P(ROW, COL),
        P(ROW, COL),
        P(COL, ROW),
    )
    out_specs = (P(COL, ROW), P(COL, ROW), P(ROW, COL), P(ROW, COL), P(COL, ROW))
    return jax.shard_map(layer, mesh=fine, in_specs=in_specs, out_specs=out_specs, check_vma=False)
```

```python
import jax
import jax.numpy as jnp
from jax import lax
from jax.experimental import pallas as pl
from jax.experimental.pallas import tpu as pltpu
from jax.sharding import Mesh
from jax.sharding import PartitionSpec as P


ROW = ("x_lo", "y", "core")
COL = ("x_hi", "z")
PAIR = ("x_lo", "y")
BF = jnp.bfloat16
F32 = jnp.float32
BLK = 128
STEP = 256


def local_call(kernel, mib, outs, *args, place=None, scratch=(), far=0):
    whole = pl.BlockSpec(memory_space=pltpu.VMEM)
    single = not isinstance(outs, list)
    first = [] if place is None else [place]
    specs = [whole] * (len(args) - far) + [pl.BlockSpec(memory_space=pl.ANY)] * far
    return pl.pallas_call(
        kernel,
        out_shape=outs,
        in_specs=[pl.BlockSpec(memory_space=pltpu.SMEM)] * len(first) + specs,
        out_specs=whole if single else [whole] * len(outs),
        scratch_shapes=scratch,
        compiler_params=pltpu.CompilerParams(vmem_limit_bytes=mib << 20),
    )(*first, *args)


def nn(left, right):
    return jnp.dot(left, right, preferred_element_type=F32)


def nt(left, right):
    return lax.dot_general(left, right, (((1,), (1,)), ((), ())), preferred_element_type=F32)


def prepare_kernel(*refs):
    for weight, mask, eff in zip(refs[0:3], refs[3:6], refs[6:9]):
        for i in range(mask.shape[0]):
            rows = pl.ds(i * BLK, BLK)
            keep = jnp.broadcast_to(mask[pl.ds(i, 1), :], (BLK, mask.shape[1])).astype(BF)
            eff[rows, :] = weight[rows, :] * keep


def partial_sums(place, own, cross, effs, effs_x, product):
    tokens, width = own.shape
    hid = max(effs[0].shape)
    n = len(effs)
    chips = place.shape[0]
    share = tokens // chips

    def kernel(place, own, cross, *refs):
        sources, outs, (left, left_x), held, sems = (
            refs[: 2 * n],
            refs[2 * n : 2 * n + chips],
            refs[2 * n + chips : 2 * n + chips + 2],
            refs[2 * n + chips + 2 : -1],
            refs[-1],
        )
        copies = [
            pltpu.make_async_copy(source, hold, sems.at[i])
            for i, (source, hold) in enumerate(zip(sources, held))
        ]
        for copy in copies:
            copy.start()
        for r in range(chips):
            source = pl.ds(pl.multiple_of(place[r] * share, share), share)
            left[pl.ds(r * share, share), :] = own[source, :]
            left_x[pl.ds(r * share, share), :] = cross[source, :]
        for part in range(n):
            copies[2 * part].wait()
            copies[2 * part + 1].wait()
            weight, weight_x = held[2 * part], held[2 * part + 1]
            for j in range(hid // STEP):
                here = pl.ds(j * STEP, STEP)
                at = (slice(None), here) if product is nn else (here, slice(None))
                value = product(left[...], weight[at]) + product(left_x[...], weight_x[at])
                for r, out in enumerate(outs):
                    out[part, :, here] = value[r * share : (r + 1) * share].astype(out.dtype)

    outs = [jax.ShapeDtypeStruct((n, share, hid), F32 if r == 0 else BF) for r in range(chips)]
    weights = [weight for two in zip(effs, effs_x) for weight in two]
    scratch = [pltpu.VMEM((tokens, width), BF)] * 2
    scratch += [pltpu.VMEM(weight.shape, BF) for weight in weights]
    scratch += [pltpu.SemaphoreType.DMA((2 * n,))]
    return local_call(
        kernel, 20, outs, own, cross, *weights, place=place, scratch=scratch, far=2 * n
    )


def activation_kernel(*refs):
    got, got_back, out = refs[:8], refs[8:16], refs[16]
    hid = out.shape[2]

    def total(group, part, cols):
        acc = group[0][part, :, cols]
        for ref in group[1:]:
            acc = acc + ref[part, :, cols].astype(F32)
        return acc

    for j in range(hid // STEP):
        cols = pl.ds(j * STEP, STEP)
        gate, up, d_hidden = total(got, 0, cols), total(got, 1, cols), total(got_back, 0, cols)
        sigmoid = jax.nn.sigmoid(gate)
        activated = gate * sigmoid
        out[0, :, cols] = (activated * up).astype(BF)
        out[1, :, cols] = (
            d_hidden * up * sigmoid * (1.0 + gate * (1.0 - sigmoid))
        ).astype(BF)
        out[2, :, cols] = (d_hidden * activated).astype(BF)


def results(acts, weights, out, ready=lambda i: None):
    down, gate, up = weights
    width = gate.shape[0]
    ready(0)
    out[:, :width] = nn(acts[0], down[...]).astype(BF)
    ready(1)
    value = nt(acts[1], gate[...])
    ready(2)
    out[:, width:] = (value + nt(acts[2], up[...])).astype(BF)


def early_kernel(*refs):
    shares, sources, (acts, away, here), held, sems = (
        refs[:4],
        refs[4:10],
        refs[10:13],
        refs[13:19],
        refs[19],
    )
    share = shares[0].shape[1]
    copies = [
        pltpu.make_async_copy(source, hold, sems.at[i])
        for i, (source, hold) in enumerate(zip(sources, held))
    ]
    for copy in copies:
        copy.start()
    for i, ref in enumerate(shares):
        acts[:, pl.ds(i * share, share), :] = ref[...]
    results(acts, held[:3], away, lambda i: copies[i].wait())
    results(acts, held[3:], here, lambda i: copies[3 + i].wait())


def late_away_kernel(*refs):
    shares, weights, (acts, away) = refs[:6], refs[6:9], refs[9:]
    share, hid = shares[0].shape[1], acts.shape[2]
    for i in range(2):
        acts[:, pl.ds(i * share, share), :] = shares[i][...]
        rows = pl.ds((2 + i) * share, share)
        acts[:, rows, : hid // 2] = shares[2 + 2 * i][...]
        acts[:, rows, hid // 2 :] = shares[3 + 2 * i][...]
    results(acts, weights, away)


def late_here_kernel(acts, *refs):
    results(acts, refs[:3], refs[3])


EARLY = (0, 4, 1, 3)
LATE = (5, 7, 2, 6)


def assemble_kernel(place, here_early, here_late, away_early, away_late, send):
    half = send.shape[1] // 2
    for order, here, away in ((EARLY, here_early, away_early), (LATE, here_late, away_late)):
        for i, r in enumerate(order):
            for k in range(2):
                rows = pl.ds((2 * i + k) * half, half)
                send[2 * place[r] + k, :half, :] = here[rows, :]
                send[2 * place[r] + k, half:, :] = away[rows, :]


def gradient_kernel(place, *refs):
    early, late, early_x, late_x = refs[:4]
    sources, masks = refs[4:8], refs[8:11]
    grad_gate, grad_up, grad_down = refs[11:14]
    moved = refs[14:]
    width, hid = grad_gate.shape
    share = sources[0].shape[0] // place.shape[0]
    for source, target in zip(sources, moved):
        for i, r in enumerate(EARLY + LATE):
            rows = pl.ds(pl.multiple_of(place[r] * share, share), share)
            target[pl.ds(i * share, share), :] = source[rows, :]
    rows, rows_x = moved[0][...].T, moved[1][...].T
    cot, cot_x = moved[2][...], moved[3][...]
    for j in range(hid // STEP):
        here = pl.ds(j * STEP, STEP)

        def all_rows(first, second, part):
            return jnp.concatenate([first[part, :, here], second[part, :, here]], axis=0)

        for part, mask, grad in ((1, masks[0], grad_gate), (2, masks[1], grad_up)):
            value = nn(rows, all_rows(early, late, part))
            value += nn(rows_x, all_rows(early_x, late_x, part))
            for i in range(width // BLK):
                keep = mask[pl.ds(i, 1), here]
                grad[pl.ds(i * BLK, BLK), here] = (value[i * BLK : (i + 1) * BLK] * keep).astype(BF)
        value = nn(all_rows(early, late, 0).T, cot) + nn(all_rows(early_x, late_x, 0).T, cot_x)
        for i in range(STEP // BLK):
            keep = masks[2][pl.ds(j * (STEP // BLK) + i, 1), :]
            grad_down[pl.ds(j * STEP + i * BLK, BLK), :] = (
                value[i * BLK : (i + 1) * BLK] * keep
            ).astype(BF)


def swap(array):
    return lax.ppermute(array, "core", [(0, 1), (1, 0)])


def layer(
    tokens, cotangent, gate_weight, up_weight, down_weight, gate_mask, up_mask, down_mask
):
    share, width = tokens.shape
    hid = gate_weight.shape[1]
    core = lax.axis_index("core")
    pairs = lax.axis_size(PAIR)
    cols = lax.axis_size(COL)
    half = share // 2

    x_lo, y = lax.axis_index("x_lo"), lax.axis_index("y")
    y_n = lax.axis_size("y")
    place = jnp.stack(
        [(x_lo ^ (r // y_n)) * y_n + (y + r % y_n) % y_n for r in range(pairs)]
    ).astype(jnp.int32)

    def gather(array):
        return lax.all_to_all(
            jnp.broadcast_to(array, (cols,) + array.shape), COL, 0, 0, tiled=True
        )

    def by_core(gathered):
        own = lax.dynamic_slice_in_dim(gathered, core * half, half, 1)
        other = lax.dynamic_slice_in_dim(gathered, (1 - core) * half, half, 1)
        return own.reshape(-1, width), other.reshape(-1, width)

    def spread(parts):
        got = {0: parts[0]}
        for r in (6, 5, 7, 2, 4, 1, 3):
            moves = [
                (i, ((i // y_n) ^ (r // y_n)) * y_n + (i % y_n + r % y_n) % y_n)
                for i in range(pairs)
            ]
            got[r] = lax.ppermute(parts[r], PAIR, moves)
        return [got[r] for r in range(pairs)]

    gathered = gather(tokens)
    weights = (gate_weight, up_weight, down_weight)
    shapes = [jax.ShapeDtypeStruct(weight.shape, BF) for weight in weights]
    wide = [
        jnp.repeat(mask.astype(F32), BLK, axis=1) for mask in (gate_mask, up_mask, down_mask)
    ]
    effs = local_call(prepare_kernel, 20, shapes, *weights, *wide)
    effs_x = [swap(eff) for eff in effs]

    gathered, cot_in = lax.optimization_barrier((gathered, cotangent))
    gathered_cot = gather(cot_in)
    own, other = by_core(gathered)
    parts = partial_sums(place, own, swap(other), effs[:2], effs_x[:2], nn)
    got = spread(parts)
    own_cot, other_cot = by_core(gathered_cot)
    back = partial_sums(place, own_cot, swap(other_cot), effs[2:], effs_x[2:], nt)
    got_back = spread(back)
    mine = local_call(
        activation_kernel,
        12,
        jax.ShapeDtypeStruct((3, parts[0].shape[1], hid), BF),
        *got,
        *got_back,
    )

    def from_up(array):
        return lax.ppermute(array, "y", [(i, (i - 1) % y_n) for i in range(y_n)])

    def from_down(array):
        return lax.ppermute(array, "y", [(i, (i + 1) % y_n) for i in range(y_n)])

    mid = hid // 2
    up_one, down_one = from_up(mine), from_down(mine)
    facing = lax.ppermute(mine, "x_lo", [(0, 1), (1, 0)])
    distant = [from_up(up_one[:, :, :mid]), from_down(down_one[:, :, mid:])]
    facing_up, facing_down = from_up(facing), from_down(facing)
    distant += [from_up(facing_up[:, :, :mid]), from_down(facing_down[:, :, mid:])]

    rows_n = own.shape[0] // 2
    acts_shape = jax.ShapeDtypeStruct((3, rows_n, hid), BF)
    sums_shape = jax.ShapeDtypeStruct((rows_n, 2 * width), BF)
    ordered = [effs_x[2], *effs_x[:2], effs[2], *effs[:2]]
    early, away_early, here_early, *resident = local_call(
        early_kernel,
        24,
        [acts_shape, sums_shape, sums_shape]
        + [pltpu.VMEM(weight.shape, BF) for weight in ordered],
        mine,
        facing,
        up_one,
        down_one,
        *ordered,
        scratch=[pltpu.SemaphoreType.DMA((6,))],
        far=6,
    )
    late, away_late = local_call(
        late_away_kernel,
        16,
        [acts_shape, sums_shape],
        facing_up,
        facing_down,
        *distant,
        *resident[:3],
    )
    away_early, away_late = swap(away_early), swap(away_late)
    here_late = local_call(late_here_kernel, 12, sums_shape, late, *resident[3:])
    send = local_call(
        assemble_kernel,
        8,
        jax.ShapeDtypeStruct((cols, share, 2 * width), BF),
        here_early,
        here_late,
        away_early,
        away_late,
        place=place,
    )
    arrived = lax.all_to_all(send, COL, 0, 0, tiled=True)
    sums = jnp.sum(arrived.astype(F32), axis=0)
    first, second = sums[:half], sums[half:]
    sums = jnp.concatenate(
        [jnp.where(core == 0, first, second), jnp.where(core == 0, second, first)], axis=0
    ).astype(BF)
    output, d_tokens = sums[:, :width], sums[:, width:]

    send, early, late = lax.optimization_barrier((send, early, late))
    grad_gate, grad_up, grad_down = local_call(
        gradient_kernel,
        20,
        shapes,
        early,
        late,
        swap(early),
        swap(late),
        own,
        other,
        own_cot,
        other_cot,
        *wide,
        place=place,
        scratch=[pltpu.VMEM(own.shape, BF)] * 4,
    )
    return (output, d_tokens, grad_gate, grad_up, grad_down)


def solution(mesh):
    fine = Mesh(mesh.devices.reshape(2, 4, 2, 2, 8), ROW + COL)
    in_specs = (
        P(COL, ROW),
        P(COL, ROW),
        P(ROW, COL),
        P(ROW, COL),
        P(COL, ROW),
        P(ROW, COL),
        P(ROW, COL),
        P(COL, ROW),
    )
    out_specs = (P(COL, ROW), P(COL, ROW), P(ROW, COL), P(ROW, COL), P(COL, ROW))
    return jax.shard_map(layer, mesh=fine, in_specs=in_specs, out_specs=out_specs, check_vma=False)
```

```python
import jax
import jax.numpy as jnp
from jax import lax
from jax.experimental import pallas as pl
from jax.experimental.pallas import tpu as pltpu
from jax.sharding import Mesh
from jax.sharding import PartitionSpec as P


ROW = ("x_lo", "y", "core")
COL = ("x_hi", "z")
PAIR = ("x_lo", "y")
BF = jnp.bfloat16
F32 = jnp.float32
BLK = 128
STEP = 256


def local_call(kernel, mib, outs, *args, place=None, scratch=(), far=0):
    whole = pl.BlockSpec(memory_space=pltpu.VMEM)
    single = not isinstance(outs, list)
    first = [] if place is None else [place]
    specs = [whole] * (len(args) - far) + [pl.BlockSpec(memory_space=pl.ANY)] * far
    return pl.pallas_call(
        kernel,
        out_shape=outs,
        in_specs=[pl.BlockSpec(memory_space=pltpu.SMEM)] * len(first) + specs,
        out_specs=whole if single else [whole] * len(outs),
        scratch_shapes=scratch,
        compiler_params=pltpu.CompilerParams(vmem_limit_bytes=mib << 20),
    )(*first, *args)


def nn(left, right):
    return jnp.dot(left, right, preferred_element_type=F32)


def nt(left, right):
    return lax.dot_general(left, right, (((1,), (1,)), ((), ())), preferred_element_type=F32)


def prepare_kernel(*refs):
    for weight, mask, eff in zip(refs[0:3], refs[3:6], refs[6:9]):
        for i in range(mask.shape[0]):
            rows = pl.ds(i * BLK, BLK)
            keep = jnp.broadcast_to(mask[pl.ds(i, 1), :], (BLK, mask.shape[1])).astype(BF)
            eff[rows, :] = weight[rows, :] * keep


def partial_sums(place, own, cross, effs, effs_x, product):
    tokens, width = own.shape
    hid = max(effs[0].shape)
    n = len(effs)
    chips = place.shape[0]
    share = tokens // chips

    def kernel(place, own, cross, *refs):
        sources, outs, (left, left_x), held, sems = (
            refs[: 2 * n],
            refs[2 * n : 2 * n + chips],
            refs[2 * n + chips : 2 * n + chips + 2],
            refs[2 * n + chips + 2 : -1],
            refs[-1],
        )
        copies = [
            pltpu.make_async_copy(source, hold, sems.at[i])
            for i, (source, hold) in enumerate(zip(sources, held))
        ]
        for copy in copies:
            copy.start()
        for r in range(chips):
            source = pl.ds(pl.multiple_of(place[r] * share, share), share)
            left[pl.ds(r * share, share), :] = own[source, :]
            left_x[pl.ds(r * share, share), :] = cross[source, :]
        for part in range(n):
            copies[2 * part].wait()
            copies[2 * part + 1].wait()
            weight, weight_x = held[2 * part], held[2 * part + 1]
            for j in range(hid // STEP):
                here = pl.ds(j * STEP, STEP)
                at = (slice(None), here) if product is nn else (here, slice(None))
                value = product(left[...], weight[at]) + product(left_x[...], weight_x[at])
                for r, out in enumerate(outs):
                    out[part, :, here] = value[r * share : (r + 1) * share].astype(out.dtype)

    outs = [jax.ShapeDtypeStruct((n, share, hid), F32 if r == 0 else BF) for r in range(chips)]
    weights = [weight for two in zip(effs, effs_x) for weight in two]
    scratch = [pltpu.VMEM((tokens, width), BF)] * 2
    scratch += [pltpu.VMEM(weight.shape, BF) for weight in weights]
    scratch += [pltpu.SemaphoreType.DMA((2 * n,))]
    return local_call(
        kernel, 20, outs, own, cross, *weights, place=place, scratch=scratch, far=2 * n
    )


def total(group, part, cols):
    acc = group[0][part, :, cols]
    for ref in group[1:]:
        acc = acc + ref[part, :, cols].astype(F32)
    return acc


def sum_kernel(*refs):
    got, out = refs[:-1], refs[-1]
    for part in range(out.shape[0]):
        for j in range(out.shape[2] // STEP):
            cols = pl.ds(j * STEP, STEP)
            out[part, :, cols] = total(got, part, cols)


def activation_kernel(forward, *refs):
    got_back, out = refs[:-1], refs[-1]
    hid = out.shape[2]
    for j in range(hid // STEP):
        cols = pl.ds(j * STEP, STEP)
        gate, up, d_hidden = forward[0, :, cols], forward[1, :, cols], total(got_back, 0, cols)
        sigmoid = jax.nn.sigmoid(gate)
        activated = gate * sigmoid
        out[0, :, cols] = (activated * up).astype(BF)
        out[1, :, cols] = (
            d_hidden * up * sigmoid * (1.0 + gate * (1.0 - sigmoid))
        ).astype(BF)
        out[2, :, cols] = (d_hidden * activated).astype(BF)


def results(acts, weights, out, ready=lambda i: None):
    down, gate, up = weights
    width = gate.shape[0]
    ready(0)
    out[:, :width] = nn(acts[0], down[...]).astype(BF)
    ready(1)
    value = nt(acts[1], gate[...])
    ready(2)
    out[:, width:] = (value + nt(acts[2], up[...])).astype(BF)


def early_kernel(*refs):
    shares, sources, (acts, away, here), held, sems = (
        refs[:4],
        refs[4:10],
        refs[10:13],
        refs[13:19],
        refs[19],
    )
    share = shares[0].shape[1]
    copies = [
        pltpu.make_async_copy(source, hold, sems.at[i])
        for i, (source, hold) in enumerate(zip(sources, held))
    ]
    for copy in copies:
        copy.start()
    for i, ref in enumerate(shares):
        acts[:, pl.ds(i * share, share), :] = ref[...]
    results(acts, held[:3], away, lambda i: copies[i].wait())
    results(acts, held[3:], here, lambda i: copies[3 + i].wait())


def late_away_kernel(*refs):
    shares, weights, (acts, away) = refs[:6], refs[6:9], refs[9:]
    share, hid = shares[0].shape[1], acts.shape[2]
    for i in range(2):
        acts[:, pl.ds(i * share, share), :] = shares[i][...]
        rows = pl.ds((2 + i) * share, share)
        acts[:, rows, : hid // 2] = shares[2 + 2 * i][...]
        acts[:, rows, hid // 2 :] = shares[3 + 2 * i][...]
    results(acts, weights, away)


def late_here_kernel(acts, *refs):
    results(acts, refs[:3], refs[3])


EARLY = (0, 4, 1, 3)
LATE = (5, 7, 2, 6)


def assemble_kernel(place, here_early, here_late, away_early, away_late, send):
    half = send.shape[1] // 2
    for order, here, away in ((EARLY, here_early, away_early), (LATE, here_late, away_late)):
        for i, r in enumerate(order):
            for k in range(2):
                rows = pl.ds((2 * i + k) * half, half)
                send[2 * place[r] + k, :half, :] = here[rows, :]
                send[2 * place[r] + k, half:, :] = away[rows, :]


def finish_kernel(place, arrived, *outs):
    half = arrived.shape[1] // 2
    width = outs[0].shape[1]
    starts = (place[0] * half, (1 - place[0]) * half)
    for which, out in enumerate(outs):
        for j in range(width // STEP):
            cols = pl.ds(which * width + j * STEP, STEP)
            acc = arrived[0, :, cols].astype(F32)
            for i in range(1, arrived.shape[0]):
                acc = acc + arrived[i, :, cols].astype(F32)
            for k, start in enumerate(starts):
                rows = pl.ds(pl.multiple_of(start, half), half)
                out[rows, pl.ds(j * STEP, STEP)] = acc[k * half : (k + 1) * half].astype(BF)


def gradient_kernel(place, *refs):
    early, late, early_x, late_x = refs[:4]
    sources, masks = refs[4:8], refs[8:11]
    grad_gate, grad_up, grad_down = refs[11:14]
    moved = refs[14:]
    width, hid = grad_gate.shape
    share = sources[0].shape[0] // place.shape[0]
    for source, target in zip(sources, moved):
        for i, r in enumerate(EARLY + LATE):
            rows = pl.ds(pl.multiple_of(place[r] * share, share), share)
            target[pl.ds(i * share, share), :] = source[rows, :]
    rows, rows_x = moved[0][...].T, moved[1][...].T
    cot, cot_x = moved[2][...], moved[3][...]
    for j in range(hid // STEP):
        here = pl.ds(j * STEP, STEP)

        def all_rows(first, second, part):
            return jnp.concatenate([first[part, :, here], second[part, :, here]], axis=0)

        for part, mask, grad in ((1, masks[0], grad_gate), (2, masks[1], grad_up)):
            value = nn(rows, all_rows(early, late, part))
            value += nn(rows_x, all_rows(early_x, late_x, part))
            for i in range(width // BLK):
                keep = mask[pl.ds(i, 1), here]
                grad[pl.ds(i * BLK, BLK), here] = (value[i * BLK : (i + 1) * BLK] * keep).astype(BF)
        value = nn(all_rows(early, late, 0).T, cot) + nn(all_rows(early_x, late_x, 0).T, cot_x)
        for i in range(STEP // BLK):
            keep = masks[2][pl.ds(j * (STEP // BLK) + i, 1), :]
            grad_down[pl.ds(j * STEP + i * BLK, BLK), :] = (
                value[i * BLK : (i + 1) * BLK] * keep
            ).astype(BF)


def swap(array):
    return lax.ppermute(array, "core", [(0, 1), (1, 0)])


def layer(
    tokens, cotangent, gate_weight, up_weight, down_weight, gate_mask, up_mask, down_mask
):
    share, width = tokens.shape
    hid = gate_weight.shape[1]
    core = lax.axis_index("core")
    pairs = lax.axis_size(PAIR)
    cols = lax.axis_size(COL)
    half = share // 2

    x_lo, y = lax.axis_index("x_lo"), lax.axis_index("y")
    y_n = lax.axis_size("y")
    place = jnp.stack(
        [(x_lo ^ (r // y_n)) * y_n + (y + r % y_n) % y_n for r in range(pairs)]
    ).astype(jnp.int32)

    def copies(array):
        return jnp.broadcast_to(array, (cols,) + array.shape)

    def gather(array):
        return lax.all_to_all(array, COL, 0, 0, tiled=True)

    def by_core(gathered):
        own = lax.dynamic_slice_in_dim(gathered, core * half, half, 1)
        other = lax.dynamic_slice_in_dim(gathered, (1 - core) * half, half, 1)
        return own.reshape(-1, width), other.reshape(-1, width)

    def spread(parts):
        got = {0: parts[0]}
        for r in (6, 5, 7, 2, 4, 1, 3):
            moves = [
                (i, ((i // y_n) ^ (r // y_n)) * y_n + (i % y_n + r % y_n) % y_n)
                for i in range(pairs)
            ]
            got[r] = lax.ppermute(parts[r], PAIR, moves)
        return [got[r] for r in range(pairs)]

    gathered = gather(copies(tokens))
    weights = (gate_weight, up_weight, down_weight)
    shapes = [jax.ShapeDtypeStruct(weight.shape, BF) for weight in weights]
    wide = [
        jnp.repeat(mask.astype(F32), BLK, axis=1) for mask in (gate_mask, up_mask, down_mask)
    ]
    effs = local_call(prepare_kernel, 20, shapes, *weights, *wide)
    effs_x = [swap(eff) for eff in effs]

    gathered, cot_in = lax.optimization_barrier((gathered, copies(cotangent)))
    gathered_cot = gather(cot_in)
    own, other = by_core(gathered)
    parts = partial_sums(place, own, swap(other), effs[:2], effs_x[:2], nn)
    got = spread(parts)
    own_cot, other_cot = by_core(gathered_cot)
    back = partial_sums(place, own_cot, swap(other_cot), effs[2:], effs_x[2:], nt)
    got_back = spread(back)
    forward = local_call(sum_kernel, 12, jax.ShapeDtypeStruct(parts[0].shape, F32), *got)
    mine = local_call(
        activation_kernel,
        12,
        jax.ShapeDtypeStruct((3, parts[0].shape[1], hid), BF),
        forward,
        *got_back,
    )

    def from_up(array):
        return lax.ppermute(array, "y", [(i, (i - 1) % y_n) for i in range(y_n)])

    def from_down(array):
        return lax.ppermute(array, "y", [(i, (i + 1) % y_n) for i in range(y_n)])

    mid = hid // 2
    up_one, down_one = from_up(mine), from_down(mine)
    facing = lax.ppermute(mine, "x_lo", [(0, 1), (1, 0)])
    distant = [from_up(up_one[:, :, :mid]), from_down(down_one[:, :, mid:])]
    facing_up, facing_down = from_up(facing), from_down(facing)
    distant += [from_up(facing_up[:, :, :mid]), from_down(facing_down[:, :, mid:])]

    rows_n = own.shape[0] // 2
    acts_shape = jax.ShapeDtypeStruct((3, rows_n, hid), BF)
    sums_shape = jax.ShapeDtypeStruct((rows_n, 2 * width), BF)
    ordered = [effs_x[2], *effs_x[:2], effs[2], *effs[:2]]
    early, away_early, here_early, *resident = local_call(
        early_kernel,
        24,
        [acts_shape, sums_shape, sums_shape]
        + [pltpu.VMEM(weight.shape, BF) for weight in ordered],
        mine,
        facing,
        up_one,
        down_one,
        *ordered,
        scratch=[pltpu.SemaphoreType.DMA((6,))],
        far=6,
    )
    late, away_late = local_call(
        late_away_kernel,
        16,
        [acts_shape, sums_shape],
        facing_up,
        facing_down,
        *distant,
        *resident[:3],
    )
    away_early, away_late = swap(away_early), swap(away_late)
    here_late = local_call(late_here_kernel, 12, sums_shape, late, *resident[3:])
    send = local_call(
        assemble_kernel,
        8,
        jax.ShapeDtypeStruct((cols, share, 2 * width), BF),
        here_early,
        here_late,
        away_early,
        away_late,
        place=place,
    )
    arrived = lax.all_to_all(send, COL, 0, 0, tiled=True)
    output, d_tokens = local_call(
        finish_kernel,
        8,
        [jax.ShapeDtypeStruct(tokens.shape, BF)] * 2,
        arrived,
        place=core.reshape(1),
    )

    send, early, late = lax.optimization_barrier((send, early, late))
    grad_gate, grad_up, grad_down = local_call(
        gradient_kernel,
        20,
        shapes,
        early,
        late,
        swap(early),
        swap(late),
        own,
        other,
        own_cot,
        other_cot,
        *wide,
        place=place,
        scratch=[pltpu.VMEM(own.shape, BF)] * 4,
    )
    return (output, d_tokens, grad_gate, grad_up, grad_down)


def solution(mesh):
    fine = Mesh(mesh.devices.reshape(2, 4, 2, 2, 8), ROW + COL)
    in_specs = (
        P(COL, ROW),
        P(COL, ROW),
        P(ROW, COL),
        P(ROW, COL),
        P(COL, ROW),
        P(ROW, COL),
        P(ROW, COL),
        P(COL, ROW),
    )
    out_specs = (P(COL, ROW), P(COL, ROW), P(ROW, COL), P(ROW, COL), P(COL, ROW))
    return jax.shard_map(layer, mesh=fine, in_specs=in_specs, out_specs=out_specs, check_vma=False)
```

```python
import jax
import jax.numpy as jnp
from jax import lax
from jax.experimental import pallas as pl
from jax.experimental.pallas import tpu as pltpu
from jax.sharding import Mesh
from jax.sharding import PartitionSpec as P


ROW = ("x_lo", "y", "core")
COL = ("x_hi", "z")
PAIR = ("x_lo", "y")
BF = jnp.bfloat16
F32 = jnp.float32
BLK = 128
STEP = 256


def local_call(kernel, mib, outs, *args, place=None, scratch=(), far=0):
    whole = pl.BlockSpec(memory_space=pltpu.VMEM)
    single = not isinstance(outs, list)
    first = [] if place is None else [place]
    specs = [whole] * (len(args) - far) + [pl.BlockSpec(memory_space=pl.ANY)] * far
    return pl.pallas_call(
        kernel,
        out_shape=outs,
        in_specs=[pl.BlockSpec(memory_space=pltpu.SMEM)] * len(first) + specs,
        out_specs=whole if single else [whole] * len(outs),
        scratch_shapes=scratch,
        compiler_params=pltpu.CompilerParams(vmem_limit_bytes=mib << 20),
    )(*first, *args)


def nn(left, right):
    return jnp.dot(left, right, preferred_element_type=F32)


def nt(left, right):
    return lax.dot_general(left, right, (((1,), (1,)), ((), ())), preferred_element_type=F32)


def prepare_kernel(*refs):
    for weight, mask, eff in zip(refs[0:3], refs[3:6], refs[6:9]):
        for i in range(mask.shape[0]):
            rows = pl.ds(i * BLK, BLK)
            keep = jnp.broadcast_to(mask[pl.ds(i, 1), :], (BLK, mask.shape[1])).astype(BF)
            eff[rows, :] = weight[rows, :] * keep


def partial_sums(place, own, cross, effs, effs_x, product):
    tokens, width = own.shape
    hid = max(effs[0].shape)
    n = len(effs)
    chips = place.shape[0]
    share = tokens // chips

    def kernel(place, own, cross, *refs):
        sources, outs, (left, left_x), held, sems = (
            refs[: 2 * n],
            refs[2 * n : 2 * n + chips],
            refs[2 * n + chips : 2 * n + chips + 2],
            refs[2 * n + chips + 2 : -1],
            refs[-1],
        )
        copies = [
            pltpu.make_async_copy(source, hold, sems.at[i])
            for i, (source, hold) in enumerate(zip(sources, held))
        ]
        for copy in copies:
            copy.start()
        for r in range(chips):
            source = pl.ds(pl.multiple_of(place[r] * share, share), share)
            left[pl.ds(r * share, share), :] = own[source, :]
            left_x[pl.ds(r * share, share), :] = cross[source, :]
        for part in range(n):
            copies[2 * part].wait()
            copies[2 * part + 1].wait()
            weight, weight_x = held[2 * part], held[2 * part + 1]
            for j in range(hid // STEP):
                here = pl.ds(j * STEP, STEP)
                at = (slice(None), here) if product is nn else (here, slice(None))
                value = product(left[...], weight[at]) + product(left_x[...], weight_x[at])
                for r, out in enumerate(outs):
                    out[part, :, here] = value[r * share : (r + 1) * share].astype(out.dtype)

    outs = [jax.ShapeDtypeStruct((n, share, hid), F32 if r == 0 else BF) for r in range(chips)]
    weights = [weight for two in zip(effs, effs_x) for weight in two]
    scratch = [pltpu.VMEM((tokens, width), BF)] * 2
    scratch += [pltpu.VMEM(weight.shape, BF) for weight in weights]
    scratch += [pltpu.SemaphoreType.DMA((2 * n,))]
    return local_call(
        kernel, 20, outs, own, cross, *weights, place=place, scratch=scratch, far=2 * n
    )


def total(group, part, cols):
    acc = group[0][part, :, cols]
    for ref in group[1:]:
        acc = acc + ref[part, :, cols].astype(F32)
    return acc


def copy_kernel(source, out):
    value = source[...]
    for i in range(out.shape[0]):
        out[i] = value


def sum_kernel(*refs):
    got, out = refs[:-1], refs[-1]
    for part in range(out.shape[0]):
        for j in range(out.shape[2] // STEP):
            cols = pl.ds(j * STEP, STEP)
            out[part, :, cols] = total(got, part, cols)


def activation_kernel(forward, *refs):
    got_back, out = refs[:-1], refs[-1]
    hid = out.shape[2]
    for j in range(hid // STEP):
        cols = pl.ds(j * STEP, STEP)
        gate, up, d_hidden = forward[0, :, cols], forward[1, :, cols], total(got_back, 0, cols)
        sigmoid = jax.nn.sigmoid(gate)
        activated = gate * sigmoid
        out[0, :, cols] = (activated * up).astype(BF)
        out[1, :, cols] = (
            d_hidden * up * sigmoid * (1.0 + gate * (1.0 - sigmoid))
        ).astype(BF)
        out[2, :, cols] = (d_hidden * activated).astype(BF)


def results(acts, weights, out, ready=lambda i: None):
    down, gate, up = weights
    width = gate.shape[0]
    ready(0)
    out[:, :width] = nn(acts[0], down[...]).astype(BF)
    ready(1)
    value = nt(acts[1], gate[...])
    ready(2)
    out[:, width:] = (value + nt(acts[2], up[...])).astype(BF)


def early_kernel(*refs):
    shares, sources, (acts, away, here), held, sems = (
        refs[:4],
        refs[4:10],
        refs[10:13],
        refs[13:19],
        refs[19],
    )
    share = shares[0].shape[1]
    copies = [
        pltpu.make_async_copy(source, hold, sems.at[i])
        for i, (source, hold) in enumerate(zip(sources, held))
    ]
    for copy in copies:
        copy.start()
    for i, ref in enumerate(shares):
        acts[:, pl.ds(i * share, share), :] = ref[...]
    results(acts, held[:3], away, lambda i: copies[i].wait())
    results(acts, held[3:], here, lambda i: copies[3 + i].wait())


def late_away_kernel(*refs):
    shares, weights, (acts, away) = refs[:5], refs[5:8], refs[8:]
    share, hid = shares[0].shape[1], acts.shape[2]
    for i, ref in ((0, shares[0]), (1, shares[1]), (3, shares[4])):
        acts[:, pl.ds(i * share, share), :] = ref[...]
    rows = pl.ds(2 * share, share)
    acts[:, rows, : hid // 2] = shares[2][...]
    acts[:, rows, hid // 2 :] = shares[3][...]
    results(acts, weights, away)


def late_here_kernel(acts, *refs):
    results(acts, refs[:3], refs[3])


EARLY = (0, 4, 1, 3)
LATE = (5, 7, 2, 6)


def assemble_kernel(place, here_early, here_late, away_early, away_late, send):
    half = send.shape[1] // 2
    for order, here, away in ((EARLY, here_early, away_early), (LATE, here_late, away_late)):
        for i, r in enumerate(order):
            for k in range(2):
                rows = pl.ds((2 * i + k) * half, half)
                send[2 * place[r] + k, :half, :] = here[rows, :]
                send[2 * place[r] + k, half:, :] = away[rows, :]


def finish_kernel(place, arrived, *outs):
    half = arrived.shape[1] // 2
    width = outs[0].shape[1]
    starts = (place[0] * half, (1 - place[0]) * half)
    for which, out in enumerate(outs):
        for j in range(width // STEP):
            cols = pl.ds(which * width + j * STEP, STEP)
            acc = arrived[0, :, cols].astype(F32)
            for i in range(1, arrived.shape[0]):
                acc = acc + arrived[i, :, cols].astype(F32)
            for k, start in enumerate(starts):
                rows = pl.ds(pl.multiple_of(start, half), half)
                out[rows, pl.ds(j * STEP, STEP)] = acc[k * half : (k + 1) * half].astype(BF)


def gradient_kernel(place, *refs):
    early, late, early_x, late_x = refs[:4]
    sources, masks = refs[4:8], refs[8:11]
    grad_gate, grad_up, grad_down = refs[11:14]
    moved = refs[14:]
    width, hid = grad_gate.shape
    share = sources[0].shape[0] // place.shape[0]
    for source, target in zip(sources, moved):
        for i, r in enumerate(EARLY + LATE):
            rows = pl.ds(pl.multiple_of(place[r] * share, share), share)
            target[pl.ds(i * share, share), :] = source[rows, :]
    rows, rows_x = moved[0][...].T, moved[1][...].T
    cot, cot_x = moved[2][...], moved[3][...]
    for j in range(hid // STEP):
        here = pl.ds(j * STEP, STEP)

        def all_rows(first, second, part):
            return jnp.concatenate([first[part, :, here], second[part, :, here]], axis=0)

        for part, mask, grad in ((1, masks[0], grad_gate), (2, masks[1], grad_up)):
            value = nn(rows, all_rows(early, late, part))
            value += nn(rows_x, all_rows(early_x, late_x, part))
            for i in range(width // BLK):
                keep = mask[pl.ds(i, 1), here]
                grad[pl.ds(i * BLK, BLK), here] = (value[i * BLK : (i + 1) * BLK] * keep).astype(BF)
        value = nn(all_rows(early, late, 0).T, cot) + nn(all_rows(early_x, late_x, 0).T, cot_x)
        for i in range(STEP // BLK):
            keep = masks[2][pl.ds(j * (STEP // BLK) + i, 1), :]
            grad_down[pl.ds(j * STEP + i * BLK, BLK), :] = (
                value[i * BLK : (i + 1) * BLK] * keep
            ).astype(BF)


def swap(array):
    return lax.ppermute(array, "core", [(0, 1), (1, 0)])


def layer(
    tokens, cotangent, gate_weight, up_weight, down_weight, gate_mask, up_mask, down_mask
):
    share, width = tokens.shape
    hid = gate_weight.shape[1]
    core = lax.axis_index("core")
    pairs = lax.axis_size(PAIR)
    cols = lax.axis_size(COL)
    half = share // 2

    x_lo, y = lax.axis_index("x_lo"), lax.axis_index("y")
    y_n = lax.axis_size("y")
    place = jnp.stack(
        [(x_lo ^ (r // y_n)) * y_n + (y + r % y_n) % y_n for r in range(pairs)]
    ).astype(jnp.int32)

    def copies(array):
        return local_call(copy_kernel, 8, jax.ShapeDtypeStruct((cols,) + array.shape, BF), array)

    def gather(array):
        return lax.all_to_all(array, COL, 0, 0, tiled=True)

    def by_core(gathered):
        own = lax.dynamic_slice_in_dim(gathered, core * half, half, 1)
        other = lax.dynamic_slice_in_dim(gathered, (1 - core) * half, half, 1)
        return own.reshape(-1, width), other.reshape(-1, width)

    def spread(parts):
        got = {0: parts[0]}
        for r in (6, 5, 7, 2, 4, 1, 3):
            moves = [
                (i, ((i // y_n) ^ (r // y_n)) * y_n + (i % y_n + r % y_n) % y_n)
                for i in range(pairs)
            ]
            got[r] = lax.ppermute(parts[r], PAIR, moves)
        return [got[r] for r in range(pairs)]

    gathered = gather(copies(tokens))
    weights = (gate_weight, up_weight, down_weight)
    shapes = [jax.ShapeDtypeStruct(weight.shape, BF) for weight in weights]
    wide = [
        jnp.repeat(mask.astype(F32), BLK, axis=1) for mask in (gate_mask, up_mask, down_mask)
    ]
    effs = local_call(prepare_kernel, 20, shapes, *weights, *wide)
    effs_x = [swap(eff) for eff in effs]

    gathered, cot_in = lax.optimization_barrier((gathered, copies(cotangent)))
    gathered_cot = gather(cot_in)
    own, other = by_core(gathered)
    parts = partial_sums(place, own, swap(other), effs[:2], effs_x[:2], nn)
    got = spread(parts)
    own_cot, other_cot = by_core(gathered_cot)
    back = partial_sums(place, own_cot, swap(other_cot), effs[2:], effs_x[2:], nt)
    got_back = spread(back)
    forward = local_call(sum_kernel, 12, jax.ShapeDtypeStruct(parts[0].shape, F32), *got)
    mine = local_call(
        activation_kernel,
        12,
        jax.ShapeDtypeStruct((3, parts[0].shape[1], hid), BF),
        forward,
        *got_back,
    )

    def from_up(array):
        return lax.ppermute(array, "y", [(i, (i - 1) % y_n) for i in range(y_n)])

    def from_down(array):
        return lax.ppermute(array, "y", [(i, (i + 1) % y_n) for i in range(y_n)])

    mid = hid // 2
    up_one, down_one = from_up(mine), from_down(mine)
    facing = lax.ppermute(mine, "x_lo", [(0, 1), (1, 0)])
    distant = [from_up(up_one[:, :, :mid]), from_down(down_one[:, :, mid:])]
    facing_up, facing_down = from_up(facing), from_down(facing)
    distant += [lax.ppermute(facing, "y", [(i, (i + 2) % y_n) for i in range(y_n)])]

    rows_n = own.shape[0] // 2
    acts_shape = jax.ShapeDtypeStruct((3, rows_n, hid), BF)
    sums_shape = jax.ShapeDtypeStruct((rows_n, 2 * width), BF)
    ordered = [effs_x[2], *effs_x[:2], effs[2], *effs[:2]]
    early, away_early, here_early, *resident = local_call(
        early_kernel,
        24,
        [acts_shape, sums_shape, sums_shape]
        + [pltpu.VMEM(weight.shape, BF) for weight in ordered],
        mine,
        facing,
        up_one,
        down_one,
        *ordered,
        scratch=[pltpu.SemaphoreType.DMA((6,))],
        far=6,
    )
    late, away_late = local_call(
        late_away_kernel,
        16,
        [acts_shape, sums_shape],
        facing_up,
        facing_down,
        *distant,
        *resident[:3],
    )
    away_early, away_late = swap(away_early), swap(away_late)
    here_late = local_call(late_here_kernel, 12, sums_shape, late, *resident[3:])
    send = local_call(
        assemble_kernel,
        8,
        jax.ShapeDtypeStruct((cols, share, 2 * width), BF),
        here_early,
        here_late,
        away_early,
        away_late,
        place=place,
    )
    arrived = lax.all_to_all(send, COL, 0, 0, tiled=True)
    output, d_tokens = local_call(
        finish_kernel,
        8,
        [jax.ShapeDtypeStruct(tokens.shape, BF)] * 2,
        arrived,
        place=core.reshape(1),
    )

    send, early, late = lax.optimization_barrier((send, early, late))
    grad_gate, grad_up, grad_down = local_call(
        gradient_kernel,
        20,
        shapes,
        early,
        late,
        swap(early),
        swap(late),
        own,
        other,
        own_cot,
        other_cot,
        *wide,
        place=place,
        scratch=[pltpu.VMEM(own.shape, BF)] * 4,
    )
    return (output, d_tokens, grad_gate, grad_up, grad_down)


def solution(mesh):
    fine = Mesh(mesh.devices.reshape(2, 4, 2, 2, 8), ROW + COL)
    in_specs = (
        P(COL, ROW),
        P(COL, ROW),
        P(ROW, COL),
        P(ROW, COL),
        P(COL, ROW),
        P(ROW, COL),
        P(ROW, COL),
        P(COL, ROW),
    )
    out_specs = (P(COL, ROW), P(COL, ROW), P(ROW, COL), P(ROW, COL), P(COL, ROW))
    return jax.shard_map(layer, mesh=fine, in_specs=in_specs, out_specs=out_specs, check_vma=False)
```

```python
import jax
import jax.numpy as jnp
from jax import lax
from jax.experimental import pallas as pl
from jax.experimental.pallas import tpu as pltpu
from jax.sharding import Mesh
from jax.sharding import PartitionSpec as P


ROW = ("x_lo", "y", "core")
COL = ("x_hi", "z")
PAIR = ("x_lo", "y")
BF = jnp.bfloat16
F32 = jnp.float32
BLK = 128
STEP = 256


def local_call(kernel, mib, outs, *args, place=None, scratch=(), far=0):
    whole = pl.BlockSpec(memory_space=pltpu.VMEM)
    single = not isinstance(outs, list)
    first = [] if place is None else [place]
    specs = [whole] * (len(args) - far) + [pl.BlockSpec(memory_space=pl.ANY)] * far
    return pl.pallas_call(
        kernel,
        out_shape=outs,
        in_specs=[pl.BlockSpec(memory_space=pltpu.SMEM)] * len(first) + specs,
        out_specs=whole if single else [whole] * len(outs),
        scratch_shapes=scratch,
        compiler_params=pltpu.CompilerParams(vmem_limit_bytes=mib << 20),
    )(*first, *args)


def nn(left, right):
    return jnp.dot(left, right, preferred_element_type=F32)


def nt(left, right):
    return lax.dot_general(left, right, (((1,), (1,)), ((), ())), preferred_element_type=F32)


def prepare_kernel(*refs):
    for weight, mask, eff in zip(refs[0:3], refs[3:6], refs[6:9]):
        for i in range(mask.shape[0]):
            rows = pl.ds(i * BLK, BLK)
            keep = jnp.broadcast_to(mask[pl.ds(i, 1), :], (BLK, mask.shape[1])).astype(BF)
            eff[rows, :] = weight[rows, :] * keep


def partial_sums(place, own, cross, effs, effs_x, product):
    tokens, width = own.shape
    hid = max(effs[0].shape)
    n = len(effs)
    chips = place.shape[0]
    share = tokens // chips

    def kernel(place, own, cross, *refs):
        sources, outs, (left, left_x), held, sems = (
            refs[: 2 * n],
            refs[2 * n : 2 * n + chips],
            refs[2 * n + chips : 2 * n + chips + 2],
            refs[2 * n + chips + 2 : -1],
            refs[-1],
        )
        copies = [
            pltpu.make_async_copy(source, hold, sems.at[i])
            for i, (source, hold) in enumerate(zip(sources, held))
        ]
        for copy in copies:
            copy.start()
        for r in range(chips):
            source = pl.ds(pl.multiple_of(place[r] * share, share), share)
            left[pl.ds(r * share, share), :] = own[source, :]
            left_x[pl.ds(r * share, share), :] = cross[source, :]
        for part in range(n):
            copies[2 * part].wait()
            copies[2 * part + 1].wait()
            weight, weight_x = held[2 * part], held[2 * part + 1]
            for j in range(hid // STEP):
                here = pl.ds(j * STEP, STEP)
                at = (slice(None), here) if product is nn else (here, slice(None))
                value = product(left[...], weight[at]) + product(left_x[...], weight_x[at])
                for r, out in enumerate(outs):
                    out[part, :, here] = value[r * share : (r + 1) * share].astype(out.dtype)

    outs = [jax.ShapeDtypeStruct((n, share, hid), F32 if r == 0 else BF) for r in range(chips)]
    weights = [weight for two in zip(effs, effs_x) for weight in two]
    scratch = [pltpu.VMEM((tokens, width), BF)] * 2
    scratch += [pltpu.VMEM(weight.shape, BF) for weight in weights]
    scratch += [pltpu.SemaphoreType.DMA((2 * n,))]
    return local_call(
        kernel, 20, outs, own, cross, *weights, place=place, scratch=scratch, far=2 * n
    )


def total(group, part, cols):
    acc = group[0][part, :, cols]
    for ref in group[1:]:
        acc = acc + ref[part, :, cols].astype(F32)
    return acc


def copy_kernel(source, out):
    value = source[...]
    for i in range(out.shape[0]):
        out[i] = value


def sum_kernel(*refs):
    got, out = refs[:-1], refs[-1]
    for part in range(out.shape[0]):
        for j in range(out.shape[2] // STEP):
            cols = pl.ds(j * STEP, STEP)
            out[part, :, cols] = total(got, part, cols)


def activation_kernel(forward, *refs):
    got_back, out = refs[:-1], refs[-1]
    hid = out.shape[2]
    for j in range(hid // STEP):
        cols = pl.ds(j * STEP, STEP)
        gate, up, d_hidden = forward[0, :, cols], forward[1, :, cols], total(got_back, 0, cols)
        sigmoid = jax.nn.sigmoid(gate)
        activated = gate * sigmoid
        out[0, :, cols] = (activated * up).astype(BF)
        out[1, :, cols] = (
            d_hidden * up * sigmoid * (1.0 + gate * (1.0 - sigmoid))
        ).astype(BF)
        out[2, :, cols] = (d_hidden * activated).astype(BF)


def results(acts, weights, out, ready=lambda i: None):
    down, gate, up = weights
    width = gate.shape[0]
    ready(0)
    out[:, :width] = nn(acts[0], down[...]).astype(BF)
    ready(1)
    value = nt(acts[1], gate[...])
    ready(2)
    out[:, width:] = (value + nt(acts[2], up[...])).astype(BF)


def early_kernel(*refs):
    shares, sources, (acts, away, here), held, sems = (
        refs[:4],
        refs[4:10],
        refs[10:13],
        refs[13:19],
        refs[19],
    )
    share = shares[0].shape[1]
    copies = [
        pltpu.make_async_copy(source, hold, sems.at[i])
        for i, (source, hold) in enumerate(zip(sources, held))
    ]
    for copy in copies:
        copy.start()
    for i, ref in enumerate(shares):
        acts[:, pl.ds(i * share, share), :] = ref[...]
    results(acts, held[:3], away, lambda i: copies[i].wait())
    results(acts, held[3:], here, lambda i: copies[3 + i].wait())


def late_away_kernel(*refs):
    shares, weights, (acts, away) = refs[:5], refs[5:8], refs[8:]
    share, hid = shares[0].shape[1], acts.shape[2]
    for i, ref in ((0, shares[0]), (1, shares[1]), (3, shares[4])):
        acts[:, pl.ds(i * share, share), :] = ref[...]
    rows = pl.ds(2 * share, share)
    acts[:, rows, : hid // 2] = shares[2][...]
    acts[:, rows, hid // 2 :] = shares[3][...]
    results(acts, weights, away)


def late_here_kernel(acts, *refs):
    results(acts, refs[:3], refs[3])


EARLY = (0, 4, 1, 3)
LATE = (5, 7, 2, 6)


def assemble_kernel(place, here_early, here_late, away_early, away_late, send):
    half = send.shape[1] // 2
    for order, here, away in ((EARLY, here_early, away_early), (LATE, here_late, away_late)):
        for i, r in enumerate(order):
            for k in range(2):
                rows = pl.ds((2 * i + k) * half, half)
                send[2 * place[r] + k, :half, :] = here[rows, :]
                send[2 * place[r] + k, half:, :] = away[rows, :]


def finish_kernel(place, arrived, *outs):
    half = arrived.shape[1] // 2
    width = outs[0].shape[1]
    starts = (place[0] * half, (1 - place[0]) * half)
    for which, out in enumerate(outs):
        for j in range(width // STEP):
            cols = pl.ds(which * width + j * STEP, STEP)
            acc = arrived[0, :, cols].astype(F32)
            for i in range(1, arrived.shape[0]):
                acc = acc + arrived[i, :, cols].astype(F32)
            for k, start in enumerate(starts):
                rows = pl.ds(pl.multiple_of(start, half), half)
                out[rows, pl.ds(j * STEP, STEP)] = acc[k * half : (k + 1) * half].astype(BF)


def gradient_kernel(place, *refs):
    early, late, early_x, late_x = refs[:4]
    sources, masks = refs[4:8], refs[8:11]
    grad_gate, grad_up, grad_down = refs[11:14]
    moved = refs[14:]
    width, hid = grad_gate.shape
    share = sources[0].shape[0] // place.shape[0]
    for source, target in zip(sources, moved):
        for i, r in enumerate(EARLY + LATE):
            rows = pl.ds(pl.multiple_of(place[r] * share, share), share)
            target[pl.ds(i * share, share), :] = source[rows, :]
    rows, rows_x = moved[0][...].T, moved[1][...].T
    cot, cot_x = moved[2][...], moved[3][...]
    for j in range(hid // STEP):
        here = pl.ds(j * STEP, STEP)

        def all_rows(first, second, part):
            return jnp.concatenate([first[part, :, here], second[part, :, here]], axis=0)

        for part, mask, grad in ((1, masks[0], grad_gate), (2, masks[1], grad_up)):
            value = nn(rows, all_rows(early, late, part))
            value += nn(rows_x, all_rows(early_x, late_x, part))
            for i in range(width // BLK):
                keep = mask[pl.ds(i, 1), here]
                grad[pl.ds(i * BLK, BLK), here] = (value[i * BLK : (i + 1) * BLK] * keep).astype(BF)
        value = nn(all_rows(early, late, 0).T, cot) + nn(all_rows(early_x, late_x, 0).T, cot_x)
        for i in range(STEP // BLK):
            keep = masks[2][pl.ds(j * (STEP // BLK) + i, 1), :]
            grad_down[pl.ds(j * STEP + i * BLK, BLK), :] = (
                value[i * BLK : (i + 1) * BLK] * keep
            ).astype(BF)


def swap(array):
    return lax.ppermute(array, "core", [(0, 1), (1, 0)])


def layer(
    tokens, cotangent, gate_weight, up_weight, down_weight, gate_mask, up_mask, down_mask
):
    share, width = tokens.shape
    hid = gate_weight.shape[1]
    core = lax.axis_index("core")
    pairs = lax.axis_size(PAIR)
    cols = lax.axis_size(COL)
    half = share // 2

    x_lo, y = lax.axis_index("x_lo"), lax.axis_index("y")
    y_n = lax.axis_size("y")
    place = jnp.stack(
        [(x_lo ^ (r // y_n)) * y_n + (y + r % y_n) % y_n for r in range(pairs)]
    ).astype(jnp.int32)

    def copies(array, axis):
        shape = (lax.axis_size(axis),) + array.shape
        return local_call(copy_kernel, 8, jax.ShapeDtypeStruct(shape, BF), array)

    def gather(array, axis):
        return lax.all_to_all(array, axis, 0, 0, tiled=True)

    def by_core(gathered):
        own = lax.dynamic_slice_in_dim(gathered, core * half, half, 1)
        other = lax.dynamic_slice_in_dim(gathered, (1 - core) * half, half, 1)
        return own.reshape(-1, width), other.reshape(-1, width)

    def spread(parts):
        got = {0: parts[0]}
        for r in (6, 5, 7, 2, 4, 1, 3):
            moves = [
                (i, ((i // y_n) ^ (r // y_n)) * y_n + (i % y_n + r % y_n) % y_n)
                for i in range(pairs)
            ]
            got[r] = lax.ppermute(parts[r], PAIR, moves)
        return [got[r] for r in range(pairs)]

    gathered = gather(copies(tokens, COL), COL)
    weights = (gate_weight, up_weight, down_weight)
    shapes = [jax.ShapeDtypeStruct(weight.shape, BF) for weight in weights]
    wide = [
        jnp.repeat(mask.astype(F32), BLK, axis=1) for mask in (gate_mask, up_mask, down_mask)
    ]
    effs = local_call(prepare_kernel, 20, shapes, *weights, *wide)
    effs_x = [swap(eff) for eff in effs]

    high = lax.axis_index("x_hi")
    cot_facing = lax.ppermute(cotangent, "x_hi", [(0, 1), (1, 0)])
    cot_pair = jnp.stack(
        [
            jnp.where(high == 0, cotangent, cot_facing),
            jnp.where(high == 0, cot_facing, cotangent),
        ]
    )
    gathered, cot_in = lax.optimization_barrier((gathered, copies(cot_pair, "z")))
    gathered_cot = gather(cot_in, "z")
    own, other = by_core(gathered)
    parts = partial_sums(place, own, swap(other), effs[:2], effs_x[:2], nn)
    got = spread(parts)
    own_cot, other_cot = by_core(
        jnp.swapaxes(gathered_cot, 0, 1).reshape(cols, share, width)
    )
    back = partial_sums(place, own_cot, swap(other_cot), effs[2:], effs_x[2:], nt)
    got_back = spread(back)
    forward = local_call(sum_kernel, 12, jax.ShapeDtypeStruct(parts[0].shape, F32), *got)
    mine = local_call(
        activation_kernel,
        12,
        jax.ShapeDtypeStruct((3, parts[0].shape[1], hid), BF),
        forward,
        *got_back,
    )

    def from_up(array):
        return lax.ppermute(array, "y", [(i, (i - 1) % y_n) for i in range(y_n)])

    def from_down(array):
        return lax.ppermute(array, "y", [(i, (i + 1) % y_n) for i in range(y_n)])

    mid = hid // 2
    up_one, down_one = from_up(mine), from_down(mine)
    facing = lax.ppermute(mine, "x_lo", [(0, 1), (1, 0)])
    distant = [from_up(up_one[:, :, :mid]), from_down(down_one[:, :, mid:])]
    facing_up, facing_down = from_up(facing), from_down(facing)
    distant += [lax.ppermute(facing, "y", [(i, (i + 2) % y_n) for i in range(y_n)])]

    rows_n = own.shape[0] // 2
    acts_shape = jax.ShapeDtypeStruct((3, rows_n, hid), BF)
    sums_shape = jax.ShapeDtypeStruct((rows_n, 2 * width), BF)
    ordered = [effs_x[2], *effs_x[:2], effs[2], *effs[:2]]
    early, away_early, here_early, *resident = local_call(
        early_kernel,
        24,
        [acts_shape, sums_shape, sums_shape]
        + [pltpu.VMEM(weight.shape, BF) for weight in ordered],
        mine,
        facing,
        up_one,
        down_one,
        *ordered,
        scratch=[pltpu.SemaphoreType.DMA((6,))],
        far=6,
    )
    late, away_late = local_call(
        late_away_kernel,
        16,
        [acts_shape, sums_shape],
        facing_up,
        facing_down,
        *distant,
        *resident[:3],
    )
    away_early, away_late = swap(away_early), swap(away_late)
    here_late = local_call(late_here_kernel, 12, sums_shape, late, *resident[3:])
    send = local_call(
        assemble_kernel,
        8,
        jax.ShapeDtypeStruct((cols, share, 2 * width), BF),
        here_early,
        here_late,
        away_early,
        away_late,
        place=place,
    )
    arrived = lax.all_to_all(send, COL, 0, 0, tiled=True)
    output, d_tokens = local_call(
        finish_kernel,
        8,
        [jax.ShapeDtypeStruct(tokens.shape, BF)] * 2,
        arrived,
        place=core.reshape(1),
    )

    send, early, late = lax.optimization_barrier((send, early, late))
    grad_gate, grad_up, grad_down = local_call(
        gradient_kernel,
        20,
        shapes,
        early,
        late,
        swap(early),
        swap(late),
        own,
        other,
        own_cot,
        other_cot,
        *wide,
        place=place,
        scratch=[pltpu.VMEM(own.shape, BF)] * 4,
    )
    return (output, d_tokens, grad_gate, grad_up, grad_down)


def solution(mesh):
    fine = Mesh(mesh.devices.reshape(2, 4, 2, 2, 8), ROW + COL)
    in_specs = (
        P(COL, ROW),
        P(COL, ROW),
        P(ROW, COL),
        P(ROW, COL),
        P(COL, ROW),
        P(ROW, COL),
        P(ROW, COL),
        P(COL, ROW),
    )
    out_specs = (P(COL, ROW), P(COL, ROW), P(ROW, COL), P(ROW, COL), P(COL, ROW))
    return jax.shard_map(layer, mesh=fine, in_specs=in_specs, out_specs=out_specs, check_vma=False)
```
